512 devices in a mesh: dp: 32 (over z, x_hi, core), seq: 16 (over y, x_lo).
Axes of the slice: x: 4 (x_hi: 2, x_lo: 2; x = x_hi * 2 + x_lo), y: 8, z: 8, core: 2. Of those that a mesh axis runs over, the one named last changes fastest.
Arguments:
- features: bfloat16 [32, 2048, 1920], P('dp', 'seq'), may hold values from -48 to 48
- segment_ids: int32 [32, 2048], P('dp'), may hold values from 0 to 7, never falling along the last dimension, each value on 1 to 512 neighbouring positions
- projections: bfloat16 [3, 1920, 1920], P(None, 'seq'), may hold values from -1 to 1
- cotangent: bfloat16 [32, 2048, 1920], P('dp', 'seq'), may hold values from -6 to 6
Outputs:
- context: bfloat16 [32, 2048, 1920], P('dp', 'seq')
- value_grad: float32 [1920, 1920], P('seq')
The draws below stay inside these ranges and needn't reach their ends.
Inputs may be any that keep to these rules, and one draw needn't show every extreme that they name: `segment_ids`: segment numbers never fall along a sequence; every utterance number appears, each utterance has 1 to 512 frames, and one has exactly 512.
All inputs are finite; a program needn't handle non-finite values.
Results may differ from the reference program's by a relative error of at most 0.011.
Values may be sent and summed in bfloat16 or wider, within the bound.
A program may use at most 64 MiB of HBM per device.

```python
import math
import jax
import jax.numpy as jnp
import numpy as np
from jax import lax

D = 1920
HEADS = 16
HEAD = 120
FRAMES = 2048
SEQS = 32
UTTS = 8
MOST = 512


def draw_features(key, part):
    base_key = jax.random.fold_in(key, 0)
    values = jnp.clip(jax.random.normal(base_key, (SEQS, FRAMES, D), jnp.float32), -6.0, 6.0)
    return values.astype(jnp.bfloat16)


def draw_projections(key, part):
    main_key = jax.random.fold_in(key, 0)
    draws = jax.random.normal(main_key, (3, D, D), jnp.float32) * D ** (-0.5)
    return jnp.clip(draws, -1.0, 1.0).astype(jnp.bfloat16)


def shard_levels(key, extent, cuts, smallest, high):
    loudness = 1.0
    for axis_at, parts in cuts:
        heights = jax.random.uniform(jax.random.fold_in(jax.random.fold_in(key, 6), axis_at), (parts,), jnp.float32, smallest / len(cuts), high / len(cuts))
        loudness = loudness * jnp.repeat(jnp.exp(heights), extent[axis_at] // parts).reshape((-1,) + (1,) * (len(extent) - 1 - axis_at))
    return loudness


def profile(count, total, most, skew):
    loads = [(1 << 20) // math.isqrt(standing ** skew) + 1 for standing in range(2, count + 1)]
    spare, given = total - most - (count - 1), [1] * (count - 1)
    while spare > 0:
        movable = [i for i in range(count - 1) if given[i] < most]
        pool, remaining = sum([loads[i] for i in movable]), spare
        for i in movable:
            more = min(most - given[i], max(1, remaining * loads[i] // pool), spare)
            given[i] = given[i] + more
            spare = spare - more
    return np.array([most] + given)


def uneven(key, count, total, most, slope):
    if count == 2:
        one = jax.random.randint(key, (), max(1, total - most), min(most, total - 1) + 1)
        return jnp.stack([one, total - one])
    sizes = jnp.asarray(profile(count, total, most, slope), jnp.int32)
    pairs = (count - 1) // 2
    giver, taker = sizes[1:1 + 2 * pairs:2], sizes[2:2 + 2 * pairs:2]
    slack = jnp.minimum(giver - 1, most - taker)
    passed = jax.random.randint(jax.random.fold_in(key, 1), (pairs,), 0, 1 << 20) % (slack + 1)
    sizes = sizes.at[1:1 + 2 * pairs:2].set(giver - passed).at[2:2 + 2 * pairs:2].set(taker + passed)
    return sizes[jax.random.permutation(jax.random.fold_in(key, 2), count)]


def noise(stream_key, shape, spread, reach, cuts=(), dtype=jnp.bfloat16):
    array = spread * jax.random.normal(stream_key, shape, jnp.float32)
    if cuts:
        array = array * shard_levels(stream_key, shape, cuts, -0.22, 0.18)
    return jnp.clip(array, -reach, reach).astype(dtype)


def setup_inputs(seed: int = 0) -> dict:
    splits = jax.random.split(jax.random.key(seed), 5)
    return {
        "features": draw_features(jax.random.fold_in(splits[4], 71), 0),
        "segment_ids": jax.vmap(lambda own: jnp.searchsorted(jnp.cumsum(uneven(own, UTTS, FRAMES, MOST, 2)), jnp.arange(FRAMES), side="right"))(jax.random.split(splits[1], SEQS)).reshape((SEQS, FRAMES)).astype(jnp.int32),
        "projections": draw_projections(jax.random.fold_in(splits[4], 71), 0),
        "cotangent": noise(splits[3], (SEQS, FRAMES, D), 1.0, 6.0, ((0, 32), (1, 16))),
    }


def reference(features, segment_ids, projections, cotangent):
    score_scale = HEAD ** -0.5

    def to_heads(matrix):
        return matrix.reshape(FRAMES, HEADS, HEAD).transpose(1, 0, 2)

    def from_heads(stacked):
        return stacked.transpose(1, 0, 2).reshape(FRAMES, D)

    def project(frames, matrix):
        return lax.dot_general(frames, matrix, (((1,), (1,)), ((), ())), preferred_element_type=jnp.float32).astype(jnp.bfloat16)

    def one_sequence(gradient_sum, sequence_item):
        frames, labels, upstream = sequence_item
        same_segment = labels[:, None] == labels[None, :]
        queries = project(frames, projections[0])
        key_rows = project(frames, projections[1])
        values = project(frames, projections[2])

        def single_head(head_item):
            head_queries, head_keys, head_values, head_upstream = head_item
            scores = jnp.dot(head_queries, head_keys.T, preferred_element_type=jnp.float32) * score_scale
            scores = jnp.where(same_segment, scores, -1e30)
            row_max = jnp.max(scores, axis=1, keepdims=True)
            exponent = jnp.exp(scores - row_max)
            attn_weights = (exponent / jnp.sum(exponent, axis=1, keepdims=True)).astype(jnp.bfloat16)
            context = jnp.dot(attn_weights, head_values, preferred_element_type=jnp.float32).astype(jnp.bfloat16)
            value_rows = jnp.dot(attn_weights.T, head_upstream, preferred_element_type=jnp.float32).astype(jnp.bfloat16)
            return context, value_rows

        context, value_rows = lax.map(single_head, (to_heads(queries), to_heads(key_rows), to_heads(values), to_heads(upstream)))
        context = from_heads(context)
        value_rows = from_heads(value_rows)
        gradient_sum = gradient_sum + jnp.dot(value_rows.T, frames, preferred_element_type=jnp.float32)
        return gradient_sum, context

    gradient_sum, context = lax.scan(one_sequence, jnp.zeros((D, D), jnp.float32), (features, segment_ids, cotangent))
    return context, gradient_sum / SEQS
```

```python
import functools

import jax
import jax.numpy as jnp
from jax import lax
from jax.experimental import pallas as pl
from jax.experimental.pallas import tpu as pltpu
from jax.sharding import PartitionSpec as P

HEAD = 120
PAD = 128
ROWS = 128
HALF = 64
WINDOW = 10
LOG2E = 1.4426950408889634
MESH = pl.DeviceIdType.MESH
NT = (((1,), (1,)), ((), ()))
NN = (((1,), (0,)), ((), ()))
TN = (((0,), (0,)), ((), ()))
F32 = jnp.float32
BF16 = jnp.bfloat16


def kernel(
    nz, feat, w, cot, seg, ctx_out, grad_out,
    G, WA, CT, DO, QKV, QS, SEGC, VRT, CX, CR, AB, AS, PB, RA, PA, RB, PC, RC, PD, RE,
    ring_s, ring_r, loc, w_s, w_r, wf_s, wf_r, qs_s, qs_r, do_s, do_r, cx_s, cx_r,
    vr_s, vr_r, a_s, a_r, b_s, b_r, c_s, c_r, d_s, d_r, e_s, e_r,
):
    ny = G.shape[0]
    ns = 2 * ny
    width = feat.shape[2]
    dp, sq = lax.axis_index("dp"), lax.axis_index("seq")
    core = lax.rem(dp, 2)
    xhi = lax.rem(lax.div(dp, 2), 2)
    z = lax.div(dp, 4)
    y = lax.div(sq, 2)
    xlo = lax.rem(sq, 2)
    peer_x = sq + 1 - 2 * xlo
    peer_core = dp + 1 - 2 * core
    peer_xhi = dp + 2 - 4 * xhi

    def remote(src, dst, ssem, rsem, dev):
        return pltpu.make_async_remote_copy(
            src_ref=src, dst_ref=dst, send_sem=ssem, recv_sem=rsem, device_id=dev, device_id_type=MESH
        )

    barrier = pltpu.get_barrier_semaphore()

    def hello(dev):
        pl.semaphore_signal(barrier, inc=1, device_id=dev, device_id_type=MESH)

    def hello_seq(d, carry):
        hello((dp, lax.rem(sq + d, ns)))
        return carry

    lax.fori_loop(1, ns, hello_seq, 0)
    hello((peer_core, sq))
    hello((peer_xhi, sq))
    hello((peer_xhi, peer_x))

    def z_dev(d):
        return lax.rem(z + d, nz) * 4 + lax.rem(dp, 4)

    def hello_z(d, carry):
        hello((z_dev(d), sq))
        return carry

    lax.fori_loop(1, nz, hello_z, 0)
    pl.semaphore_wait(barrier, ns - 1 + 3 + nz - 1)

    last = ny - 1

    def ring(dirn, k, at):
        hops = k // 2
        if dirn == 0:
            shard, half, to = lax.rem(at + ny - hops, ny), k % 2, lax.rem(sq + 2, ns)
        else:
            shard, half, to = lax.rem(at + hops, ny), 1 - k % 2, lax.rem(sq + ns - 2, ns)
        src = feat.at[half] if k < 2 else G.at[shard, half]
        return remote(src, G.at[shard, half], ring_s.at[dirn, k], ring_r.at[dirn, k], (dp, to))

    def ring_send(dirn, k):
        return ring(dirn, k, y)

    def ring_recv(dirn, k):
        return ring(dirn, k, lax.rem(y + ny - 1, ny) if dirn == 0 else lax.rem(y + 1, ny))

    for k in range(2):
        for dirn in range(2):
            ring_send(dirn, k).start()
    w_send = remote(w.at[:, core], WA.at[1, :, core], w_s, w_r, (dp, peer_x))
    w_send.start()
    own_feat = pltpu.make_async_copy(feat, G.at[y], loc.at[0])
    own_feat.start()
    own_w = pltpu.make_async_copy(w, WA.at[0], loc.at[1])
    own_w.start()

    for h in range(ns):
        CT[h] = jnp.zeros((ROWS, PAD), BF16)
        CT[h, :, 0:HEAD] = cot[:, h * HEAD : (h + 1) * HEAD]
    DO[sq] = CT[sq]

    def label_col(b, carry):
        row = seg[pl.ds(b, 1), :].astype(F32)
        SEGC[b] = jnp.broadcast_to(row, (ROWS, ROWS)).T
        return carry

    lax.fori_loop(0, ns, label_col, 0)
    VRT[...] = jnp.zeros_like(VRT)

    own_feat.wait()
    own_w.wait()

    def project(shard):
        x = G[shard].reshape(ROWS, width)
        wall = WA[...].reshape(6 * PAD, width)
        r = lax.dot_general(x, wall, NT, preferred_element_type=F32).astype(BF16)
        for p in range(3):
            QKV[2 * shard + xlo, p] = r[:, p * PAD : (p + 1) * PAD]
            QS[shard, p] = r[:, (3 + p) * PAD : (4 + p) * PAD]
        qs_copy(shard).start()

    def qs_copy(shard):
        return remote(
            QS.at[shard], QKV.at[2 * shard + xlo], qs_s.at[shard], qs_r.at[shard], (dp, peer_x)
        )

    def at_y(d):
        return lax.rem(y + d + ny, ny)

    def arrive(k):
        for dirn in range(2):
            ring_recv(dirn, k).wait_recv()
            if k + 2 <= last - 1:
                ring_send(dirn, k + 2).start()

    def do_copy(d):
        to = lax.rem(sq + d, ns)
        return remote(CT.at[to], DO.at[sq], do_s.at[to], do_r.at[sq], (dp, to))

    def do_start(t, carry):
        d = lax.rem(ny + t, ns)

        @pl.when(d != 0)
        def _():
            do_copy(d).start()

        return carry

    arrive(0)
    arrive(1)
    w_send.wait_recv()
    w_fwd = remote(WA.at[1, :, core], WA.at[1, :, core], wf_s, wf_r, (peer_core, sq))
    w_fwd.start()
    arrive(2)
    other = 1 - core
    remote(WA.at[1, :, other], WA.at[1, :, other], wf_s, wf_r, (peer_core, sq)).wait_recv()
    project(y)
    arrive(3)
    project(at_y(1))
    project(at_y(-1))
    arrive(4)
    lax.fori_loop(0, ns, do_start, 0)
    project(at_y(2))
    project(at_y(-2))
    arrive(5)
    project(at_y(3))
    project(at_y(-3))
    arrive(6)
    project(at_y(4))

    def qs_wait(t, carry):
        qs_copy(t).wait_send()
        b = 2 * t + (1 - xlo)
        remote(QS.at[t], QKV.at[b], qs_s.at[t], qs_r.at[t], (dp, peer_x)).wait_recv()
        return carry

    lax.fori_loop(0, ny, qs_wait, 0)

    scale = HEAD ** (-0.5) * LOG2E

    def do_wait(b):
        @pl.when(b != sq)
        def _():
            remote(CT.at[b], DO.at[b], do_s.at[b], do_r.at[b], (dp, b)).wait_recv()

    def cx_copy(b):
        return remote(CX.at[b], CR.at[sq], cx_s.at[b], cx_r.at[sq], (dp, b))

    def attend(t, carry):
        i = lax.rem(y + 4 + t, ny)
        s0 = jnp.clip(i - 2, 0, ny - WINDOW // 2)
        q = QKV[pl.ds(2 * i, 2), 0].reshape(2 * ROWS, PAD)
        keys = QKV[pl.ds(2 * s0, WINDOW), 1].reshape(WINDOW * ROWS, PAD)
        vals = QKV[pl.ds(2 * s0, WINDOW), 2].reshape(WINDOW * ROWS, PAD)
        s = lax.dot_general(q, keys, NT, preferred_element_type=F32)
        col = SEGC[pl.ds(2 * i, 2)].reshape(2 * ROWS, PAD)
        parts = []
        for j in range(WINDOW):
            row = seg[pl.ds(2 * s0 + j, 1), :].astype(F32)
            parts.append(jnp.where(col == row, s[:, j * PAD : (j + 1) * PAD], -1e30))
        top = functools.reduce(jnp.maximum, parts)
        top = jnp.max(top, axis=1, keepdims=True)
        es = [jnp.exp2((part - top) * scale) for part in parts]
        total = jnp.sum(functools.reduce(jnp.add, es), axis=1, keepdims=True)
        inv = 1.0 / total
        e = jnp.concatenate([part.astype(BF16) for part in es], axis=1)
        ctx = lax.dot_general(e, vals, NN, preferred_element_type=F32) * inv
        CX[pl.ds(2 * i, 2)] = ctx.astype(BF16).reshape(2, ROWS, PAD)
        for c in range(2):
            b = 2 * i + c

            @pl.when(b != sq)
            def _(b=b):
                cx_copy(b).start()

            do_wait(b)
        up = DO[pl.ds(2 * i, 2)].reshape(2 * ROWS, PAD).astype(F32) * inv
        vr = lax.dot_general(up.astype(BF16), e, TN, preferred_element_type=F32)
        for j in range(WINDOW // 2):
            VRT[s0 + j] += vr[:, j * 2 * PAD : (j + 1) * 2 * PAD]
        return carry

    lax.fori_loop(0, ny, attend, 0)
    CR[sq] = CX[sq]

    for t in range(ny):
        v = VRT[t].astype(BF16)
        left, right = v[:, :PAD], v[:, PAD:]
        AB[xlo, t] = jnp.where(xlo == 0, left, right)
        AS[t] = jnp.where(xlo == 0, right, left)
    vr_send = remote(AS, AB.at[xlo], vr_s, vr_r, (dp, peer_x))
    vr_send.start()
    remote(AS, AB.at[1 - xlo], vr_s, vr_r, (dp, peer_x)).wait_recv()

    lhs = jnp.concatenate(
        [jnp.concatenate([AB[h, t] for t in range(ny)], axis=1) for h in range(2)], axis=0
    )
    group = 512
    for g in range(4):
        lo, hi = g * group, min((g + 1) * group, width)
        rhs = G[:, :, :, lo:hi].reshape(ny * ROWS, hi - lo)
        part = lax.dot_general(lhs, rhs, NN, preferred_element_type=F32).astype(BF16)
        if hi - lo < group:
            part = jnp.concatenate([part, jnp.zeros((2 * PAD, group - (hi - lo)), BF16)], axis=1)
        for h in range(2):
            PB[g % 2, h, g // 2] = part[h * PAD : (h + 1) * PAD].reshape(8, 16, group)

    a_send = remote(PB.at[other], RA, a_s, a_r, (peer_core, sq))
    a_send.start()
    a_send.wait_recv()
    for h in range(2):
        for g in range(2):
            PA[h, g] = (PB[core, h, g].astype(F32) + RA[h, g].astype(F32)).astype(BF16)

    def b_copy(n):
        hi, lo = (xhi, 1 - xlo) if n == 0 else (1 - xhi, xlo) if n == 1 else (1 - xhi, 1 - xlo)
        dev = (dp if n == 0 else peer_xhi, sq if n == 1 else peer_x)
        return remote(PA.at[lo, hi], RB.at[n], b_s.at[n], b_r.at[n], dev)

    for n in (2, 1, 0):
        b_copy(n).start()
    for n in range(3):
        b_copy(n).wait_recv()
    total = PA[xlo, xhi].astype(F32)
    for n in range(3):
        total += RB[n].astype(F32)
    PC[...] = total.astype(BF16)

    rows = 8 // nz

    def c_copy(d):
        to = lax.rem(z + d, nz)
        return remote(
            PC.at[pl.ds(to * rows, rows)], RC.at[d], c_s.at[d], c_r.at[d], (z_dev(d), sq)
        )

    for d in range(1, nz):
        c_copy(d).start()
    total = PC[pl.ds(z * rows, rows)].astype(F32)
    for d in range(1, nz):
        c_copy(d).wait_recv()
        total += RC[d].astype(F32)
    PD[...] = total.astype(BF16)
    mine = pl.ds(z * rows, rows)
    RE[xhi, core, mine] = total.astype(BF16)

    def d_copy(d):
        return remote(PD, RE.at[xhi, core, mine], d_s.at[d], d_r.at[d], (z_dev(d), sq))

    for d in range(1, nz):
        d_copy(d).start()
    for d in range(1, nz):
        frm = lax.rem(z + nz - d, nz)
        remote(
            PD, RE.at[xhi, core, pl.ds(frm * rows, rows)], d_s.at[d], d_r.at[d], (z_dev(d), sq)
        ).wait_recv()

    def e_copy(n):
        if n == 0:
            ref, dev = RE.at[xhi, core], (peer_xhi, sq)
        elif n == 1:
            ref, dev = RE.at[xhi, core], (peer_core, sq)
        else:
            ref, dev = RE.at[1 - xhi, core], (peer_core, sq)
        return remote(ref, ref, e_s.at[n], e_r.at[n], dev)

    def e_recv(n):
        if n == 0:
            ref, dev = RE.at[1 - xhi, core], (peer_xhi, sq)
        elif n == 1:
            ref, dev = RE.at[xhi, other], (peer_core, sq)
        else:
            ref, dev = RE.at[1 - xhi, other], (peer_core, sq)
        remote(ref, ref, e_s.at[n], e_r.at[n], dev).wait_recv()

    e_copy(0).start()
    e_copy(1).start()

    def cx_wait(b, carry):
        @pl.when(b != sq)
        def _():
            remote(CX.at[b], CR.at[b], cx_s.at[b], cx_r.at[b], (dp, b)).wait_recv()
            cx_copy(b).wait_send()
            remote(CT.at[b], DO.at[sq], do_s.at[b], do_r.at[sq], (dp, b)).wait_send()

        return carry

    lax.fori_loop(0, ns, cx_wait, 0)
    for h in range(ns):
        ctx_out[:, h * HEAD : (h + 1) * HEAD] = CR[h, :, 0:HEAD]

    e_recv(0)
    e_copy(2).start()
    e_recv(1)
    e_recv(2)
    for g in range(4):
        lo, hi = g * group, min((g + 1) * group, width)
        block = RE[g // 2, g % 2].reshape(PAD, group)[:HEAD, : hi - lo]
        grad_out[:, lo:hi] = block.astype(F32) * (1.0 / (4 * nz))

    for k in range(last):
        for dirn in range(2):
            ring_send(dirn, k).wait_send()
    w_send.wait_send()
    w_fwd.wait_send()
    vr_send.wait_send()
    a_send.wait_send()
    for n in range(3):
        b_copy(n).wait_send()
        e_copy(n).wait_send()
    for d in range(1, nz):
        c_copy(d).wait_send()
        d_copy(d).wait_send()


def body(nz, features, segment_ids, projections, cotangent):
    ns = lax.axis_size("seq")
    ny = ns // 2
    width = features.shape[2]
    feat = features.reshape(2, HALF, width)
    w = jnp.pad(projections, ((0, 0), (0, PAD - HEAD), (0, 0))).reshape(3, 2, HALF, width)
    seg = segment_ids.reshape(ns, ROWS)
    vmem = lambda *shape: pltpu.VMEM(shape, BF16)
    dma = lambda *shape: pltpu.SemaphoreType.DMA(shape)
    rows = 8 // nz
    ctx, grad = pl.pallas_call(
        functools.partial(kernel, nz),
        out_shape=(
            jax.ShapeDtypeStruct((ROWS, width), BF16),
            jax.ShapeDtypeStruct((HEAD, width), F32),
        ),
        in_specs=[pl.BlockSpec(memory_space=pltpu.VMEM)] * 4,
        out_specs=[pl.BlockSpec(memory_space=pltpu.VMEM)] * 2,
        scratch_shapes=[
            vmem(ny, 2, HALF, width),
            vmem(2, 3, 2, HALF, width),
            vmem(ns, ROWS, PAD),
            vmem(ns, ROWS, PAD),
            vmem(ns, 3, ROWS, PAD),
            vmem(ny, 3, ROWS, PAD),
            pltpu.VMEM((ns, ROWS, ROWS), F32),
            pltpu.VMEM((ny, PAD, 2 * ROWS), F32),
            vmem(ns, ROWS, PAD),
            vmem(ns, ROWS, PAD),
            vmem(2, ny, PAD, ROWS),
            vmem(ny, PAD, ROWS),
            vmem(2, 2, 2, 8, 16, 512),
            vmem(2, 2, 8, 16, 512),
            vmem(2, 2, 8, 16, 512),
            vmem(3, 8, 16, 512),
            vmem(8, 16, 512),
            vmem(nz, rows, 16, 512),
            vmem(rows, 16, 512),
            vmem(2, 2, 8, 16, 512),
            dma(2, ny - 1), dma(2, ny - 1),
            dma(2),
            dma(), dma(), dma(), dma(),
            dma(ny), dma(ny),
            dma(ns), dma(ns),
            dma(ns), dma(ns),
            dma(), dma(), dma(), dma(),
            dma(3), dma(3),
            dma(nz), dma(nz),
            dma(nz), dma(nz),
            dma(3), dma(3),
        ],
        compiler_params=pltpu.CompilerParams(
            collective_id=0, has_side_effects=True, vmem_limit_bytes=60 * 1024 * 1024
        ),
    )(feat, w, cotangent[0], seg)
    return (ctx[None], grad)


def solution(mesh):
    in_specs = (P("dp", "seq", None), P("dp", None), P(None, "seq", None), P("dp", "seq", None))
    out_specs = (P("dp", "seq", None), P("seq", None))
    step = functools.partial(body, mesh.shape["dp"] // 4)
    return jax.shard_map(step, mesh=mesh, in_specs=in_specs, out_specs=out_specs, check_vma=False)
```

```python
import functools

import jax
import jax.numpy as jnp
from jax import lax
from jax.experimental import pallas as pl
from jax.experimental.pallas import tpu as pltpu
from jax.sharding import PartitionSpec as P

HEAD = 120
PAD = 128
ROWS = 128
HALF = 64
REACH = 2
STREAMS = 2
GROUP = 512
LOG2E = 1.4426950408889634
MESH = pl.DeviceIdType.MESH
NT = (((1,), (1,)), ((), ()))
NN = (((1,), (0,)), ((), ()))
TN = (((0,), (0,)), ((), ()))
F32 = jnp.float32
BF16 = jnp.bfloat16


def kernel(
    nz, feat, w, cot, seg, CR, RE,
    G, WR, WA, CO, CT, DO, QKV, QS, SEGC, EB, INV, VRT, CX, AB, AS, PB, RA, PA, RB, PC, RC, PD,
    ring_s, ring_r, loc, w_s, w_r, wz_s, wz_r, wc_s, wc_r, qs_s, qs_r, do_s, do_r, cx_s, cx_r,
    vr_s, vr_r, a_s, a_r, b_s, b_r, c_s, c_r, d_s, d_r, e_s, e_r,
):
    ny = G.shape[0]
    ns = 2 * ny
    width = feat.shape[2]
    dp, sq = lax.axis_index("dp"), lax.axis_index("seq")
    core = lax.rem(dp, 2)
    xhi = lax.rem(lax.div(dp, 2), 2)
    z = lax.div(dp, 4)
    zlo = lax.rem(z, 2)
    y = lax.div(sq, 2)
    xlo = lax.rem(sq, 2)
    other = 1 - core
    peer_x = sq + 1 - 2 * xlo
    peer_core = dp + 1 - 2 * core
    peer_xhi = dp + 2 - 4 * xhi
    peer_z = dp + 4 - 8 * zlo

    def remote(src, dst, ssem, rsem, dev):
        return pltpu.make_async_remote_copy(
            src_ref=src, dst_ref=dst, send_sem=ssem, recv_sem=rsem, device_id=dev, device_id_type=MESH
        )

    own_feat = pltpu.make_async_copy(feat, G.at[y], loc.at[0])
    own_w = pltpu.make_async_copy(w, WR, loc.at[1])
    own_cot = pltpu.make_async_copy(cot, CO, loc.at[2])
    own_feat.start()
    own_w.start()
    own_cot.start()

    barrier = pltpu.get_barrier_semaphore()

    def hello(dev):
        pl.semaphore_signal(barrier, inc=1, device_id=dev, device_id_type=MESH)

    def hello_seq(d, carry):
        hello((dp, lax.rem(sq + d, ns)))
        return carry

    lax.fori_loop(1, ns, hello_seq, 0)
    hello((peer_core, sq))
    hello((peer_xhi, sq))
    hello((peer_xhi, peer_x))

    def z_dev(d):
        return lax.rem(z + d, nz) * 4 + lax.rem(dp, 4)

    def hello_z(d, carry):
        hello((z_dev(d), sq))
        return carry

    lax.fori_loop(1, nz, hello_z, 0)

    own_w.wait()
    quarter = HALF // 2
    for p in range(3):
        for c in range(4):
            lo = c * quarter
            hi = min(lo + quarter, HEAD)
            WA[0, p, c // 2, c % 2, 0 : hi - lo] = WR[p, lo:hi]
            if hi - lo < quarter:
                WA[0, p, c // 2, c % 2, hi - lo :] = jnp.zeros((quarter - hi + lo, width), BF16)
    own_feat.wait()
    pl.semaphore_wait(barrier, ns - 1 + 3 + nz - 1)

    last = ny - 1

    def ring(dirn, k, at):
        hops = k // 2
        if dirn == 0:
            shard, half, to = lax.rem(at + ny - hops, ny), k % 2, lax.rem(sq + 2, ns)
        else:
            shard, half, to = lax.rem(at + hops, ny), 1 - k % 2, lax.rem(sq + ns - 2, ns)
        ref = G.at[shard, half]
        return remote(ref, ref, ring_s.at[dirn, k], ring_r.at[dirn, k], (dp, to))

    def ring_send(dirn, k):
        return ring(dirn, k, y)

    def ring_recv(dirn, k):
        return ring(dirn, k, lax.rem(y + ny - 1, ny) if dirn == 0 else lax.rem(y + 1, ny))

    for k in range(2):
        for dirn in range(2):
            ring_send(dirn, k).start()

    def w_x(p):
        return remote(
            WA.at[0, p, core, zlo], WA.at[1, p, core, zlo], w_s.at[p], w_r.at[p], (dp, peer_x)
        )

    def w_z(p, at):
        ref = WA.at[1, p, core, at]
        return remote(ref, ref, wz_s.at[p], wz_r.at[p], (peer_z, sq))

    def w_c(p, c, at, n):
        ref = WA.at[1, p, c, at]
        return remote(ref, ref, wc_s.at[n, p], wc_r.at[n, p], (peer_core, sq))

    for p in range(3):
        w_x(p).start()

    own_cot.wait()
    for h in range(ns):
        CT[h] = jnp.zeros((ROWS, PAD), BF16)
        CT[h, :, 0:HEAD] = CO[:, h * HEAD : (h + 1) * HEAD]
    DO[sq] = CT[sq]

    def label_col(b, carry):
        row = seg[pl.ds(b, 1), :].astype(F32)
        SEGC[b] = jnp.broadcast_to(row, (ROWS, ROWS)).T
        return carry

    lax.fori_loop(0, ns, label_col, 0)
    VRT[...] = jnp.zeros_like(VRT)

    def at_y(d):
        return lax.rem(y + d + ny, ny)

    def arrive(k):
        for dirn in range(2):
            ring_recv(dirn, k).wait_recv()
            if k + 2 <= last - 1:
                ring_send(dirn, k + 2).start()

    for p in range(3):
        w_x(p).wait_recv()
        w_z(p, zlo).start()
        w_c(p, core, zlo, 0).start()
    arrive(0)
    for p in range(3):
        w_z(p, 1 - zlo).wait_recv()
        w_c(p, core, 1 - zlo, 1).start()
    arrive(1)

    def qs_copy(shard):
        return remote(
            QS.at[shard], QKV.at[2 * shard + xlo], qs_s.at[shard], qs_r.at[shard], (dp, peer_x)
        )

    def project(shard):
        x = G[shard].reshape(ROWS, width)
        wall = WA[...].reshape(6 * PAD, width)
        r = lax.dot_general(x, wall, NT, preferred_element_type=F32).astype(BF16)
        for p in range(3):
            QS[shard, p] = r[:, (3 + p) * PAD : (4 + p) * PAD]
        qs_copy(shard).start()
        for p in range(3):
            QKV[2 * shard + xlo, p] = r[:, p * PAD : (p + 1) * PAD]

    def qs_wait(shard):
        b = 2 * shard + (1 - xlo)
        remote(
            QS.at[shard], QKV.at[b], qs_s.at[shard], qs_r.at[shard], (dp, peer_x)
        ).wait_recv()

    def do_copy(to):
        return remote(CT.at[to], DO.at[sq], do_s.at[to], do_r.at[sq], (dp, to))

    def do_start(cross):
        col = xlo + cross - 2 * cross * xlo
        for d in (4, 3, -3, 2, -2, 1, -1):
            do_copy(2 * at_y(d) + col).start()
        if cross:
            do_copy(2 * y + col).start()

    scale = HEAD ** (-0.5) * LOG2E

    def rows_of(p, r):
        return QKV[pl.ds(2 * r, 2), p].reshape(2 * ROWS, PAD)

    def attend(i):
        q = rows_of(0, i)
        col = SEGC[pl.ds(2 * i, 2)].reshape(2 * ROWS, PAD)
        parts = []
        for o in range(-REACH, REACH + 1):
            r = lax.rem(i + o + ny, ny)
            s = lax.dot_general(q, rows_of(1, r), NT, preferred_element_type=F32)
            for c in range(2):
                row = seg[pl.ds(2 * r + c, 1), :].astype(F32)
                parts.append(jnp.where(col == row, s[:, c * PAD : (c + 1) * PAD], -1e30))
        top = functools.reduce(jnp.maximum, parts)
        top = jnp.max(top, axis=1, keepdims=True)
        total = jnp.zeros((2 * ROWS, PAD), F32)
        ctx = jnp.zeros((2 * ROWS, PAD), F32)
        for n in range(2 * REACH + 1):
            left, right = (jnp.exp2((part - top) * scale) for part in parts[2 * n : 2 * n + 2])
            total += left + right
            e = jnp.concatenate([left.astype(BF16), right.astype(BF16)], axis=1)
            EB[i, n] = e
            r = lax.rem(i + n - REACH + ny, ny)
            ctx += lax.dot_general(e, rows_of(2, r), NN, preferred_element_type=F32)
        inv = jnp.broadcast_to(1.0 / jnp.sum(total, axis=1, keepdims=True), (2 * ROWS, PAD))
        INV[i] = inv
        CX[pl.ds(2 * i, 2)] = (ctx * inv).astype(BF16).reshape(2, ROWS, PAD)

    def attend_at(d, carry):
        attend(at_y(d))
        return carry

    arrive(2)
    for p in range(3):
        w_c(p, other, zlo, 0).wait_recv()
        w_c(p, other, 1 - zlo, 1).wait_recv()
    project(y)
    arrive(3)
    project(at_y(1))
    project(at_y(-1))
    arrive(4)
    do_start(0)
    project(at_y(2))
    project(at_y(-2))
    arrive(5)
    project(at_y(3))
    project(at_y(-3))
    for d in (0, 1, -1, 2, -2):
        qs_wait(at_y(d))
    attend(y)
    arrive(6)
    project(at_y(4))
    do_start(1)
    qs_wait(at_y(3))
    qs_wait(at_y(-3))
    qs_wait(at_y(4))
    lax.fori_loop(1, ny, attend_at, 0)

    def vr_copy(r):
        return remote(AS.at[r], AB.at[xlo, r], vr_s.at[r], vr_r.at[r], (dp, peer_x))

    def value_rows_out(r):
        v = VRT[r].astype(BF16)
        left, right = v[:, :PAD], v[:, PAD:]
        AS[r] = jnp.where(xlo == 0, right, left)
        vr_copy(r).start()
        AB[xlo, r] = jnp.where(xlo == 0, left, right)

    def do_wait(b):
        @pl.when(b != sq)
        def _():
            remote(CT.at[b], DO.at[b], do_s.at[b], do_r.at[b], (dp, b)).wait_recv()

    def value_step(t, carry):
        i = lax.rem(y + 4 + t, ny)
        do_wait(2 * i)
        do_wait(2 * i + 1)
        up = DO[pl.ds(2 * i, 2)].reshape(2 * ROWS, PAD).astype(F32) * INV[i]
        up = up.astype(BF16)
        for n in range(2 * REACH + 1):
            r = lax.rem(i + n - REACH + ny, ny)
            VRT[r] += lax.dot_general(up, EB[i, n], TN, preferred_element_type=F32)

        @pl.when(t >= 4)
        def _():
            value_rows_out(lax.rem(y + 2 + t, ny))

        return carry

    lax.fori_loop(0, ny, value_step, 0)
    for d in range(2, 6):
        value_rows_out(at_y(d))

    def cx_copy(b):
        return remote(CX.at[b], CR.at[sq], cx_s.at[b], cx_r.at[sq], (dp, b))

    def cx_start(d, carry):
        cx_copy(lax.rem(sq + d, ns)).start()
        return carry

    lax.fori_loop(1, ns, cx_start, 0)
    CR[sq] = CX[sq]

    for r in range(ny):
        remote(AS.at[r], AB.at[1 - xlo, r], vr_s.at[r], vr_r.at[r], (dp, peer_x)).wait_recv()
    lhs = jnp.concatenate(
        [jnp.concatenate([AB[h, t] for t in range(ny)], axis=1) for h in range(2)], axis=0
    )
    lanes = GROUP // STREAMS

    def a_copy(u):
        return remote(PB.at[u, other], RA.at[u], a_s.at[u], a_r.at[u], (peer_core, sq))

    for u in range(STREAMS):
        for g in range(4):
            lo = g * GROUP + u * lanes
            hi = min(lo + lanes, width)
            rhs = G[:, :, :, lo:hi].reshape(ny * ROWS, hi - lo)
            part = lax.dot_general(lhs, rhs, NN, preferred_element_type=F32).astype(BF16)
            if hi - lo < lanes:
                part = jnp.concatenate([part, jnp.zeros((2 * PAD, lanes - hi + lo), BF16)], axis=1)
            for h in range(2):
                PB[u, g % 2, h, g // 2] = part[h * PAD : (h + 1) * PAD].reshape(8, 16, lanes)
        a_copy(u).start()

    def b_copy(u, n):
        hi, lo = (xhi, 1 - xlo) if n == 0 else (1 - xhi, xlo) if n == 1 else (1 - xhi, 1 - xlo)
        dev = (dp if n == 0 else peer_xhi, sq if n == 1 else peer_x)
        return remote(PA.at[u, lo, hi], RB.at[u, n], b_s.at[u, n], b_r.at[u, n], dev)

    for u in range(STREAMS):
        a_copy(u).wait_recv()
        for h in range(2):
            for g in range(2):
                PA[u, h, g] = (PB[u, core, h, g].astype(F32) + RA[u, h, g].astype(F32)).astype(BF16)
        for n in (1, 2, 0):
            b_copy(u, n).start()

    rows = 8 // nz

    def c_copy(u, d):
        to = lax.rem(z + d, nz)
        return remote(
            PC.at[u, pl.ds(to * rows, rows)], RC.at[u, d], c_s.at[u, d], c_r.at[u, d], (z_dev(d), sq)
        )

    for u in range(STREAMS):
        total = PA[u, xlo, xhi].astype(F32)
        for n in range(3):
            b_copy(u, n).wait_recv()
            total += RB[u, n].astype(F32)
        PC[u] = total.astype(BF16)
        for d in range(1, nz):
            c_copy(u, d).start()

    def d_copy(u, d, frm):
        return remote(
            PD.at[u],
            RE.at[u, xhi, core, pl.ds(frm * rows, rows)],
            d_s.at[u, d],
            d_r.at[u, d],
            (z_dev(d), sq),
        )

    for u in range(STREAMS):
        total = PC[u, pl.ds(z * rows, rows)].astype(F32)
        for d in range(1, nz):
            c_copy(u, d).wait_recv()
            total += RC[u, d].astype(F32)
        PD[u] = total.astype(BF16)
        for d in range(1, nz):
            d_copy(u, d, z).start()
        RE[u, xhi, core, pl.ds(z * rows, rows)] = total.astype(BF16)

    def e_copy(u, n, recv=False):
        c = other if recv and n > 0 else core
        hi = 1 - xhi if (n == 2) != (recv and n == 0) else xhi
        ref = RE.at[u, hi, c]
        dev = (peer_xhi if n == 0 else peer_core, sq)
        return remote(ref, ref, e_s.at[u, n], e_r.at[u, n], dev)

    for u in range(STREAMS):
        for d in range(1, nz):
            d_copy(u, d, lax.rem(z + nz - d, nz)).wait_recv()
        e_copy(u, 0).start()
        e_copy(u, 1).start()

    def cx_wait(b, carry):
        @pl.when(b != sq)
        def _():
            remote(CX.at[b], CR.at[b], cx_s.at[b], cx_r.at[b], (dp, b)).wait_recv()
            cx_copy(b).wait_send()
            do_copy(b).wait_send()

        return carry

    lax.fori_loop(0, ns, cx_wait, 0)

    for u in range(STREAMS):
        e_copy(u, 0, True).wait_recv()
        e_copy(u, 2).start()

    for k in range(last):
        for dirn in range(2):
            ring_send(dirn, k).wait_send()
    for p in range(3):
        w_x(p).wait_send()
        w_z(p, zlo).wait_send()
        w_c(p, core, zlo, 0).wait_send()
        w_c(p, core, 1 - zlo, 1).wait_send()
    for r in range(ny):
        qs_copy(r).wait_send()
        vr_copy(r).wait_send()
    for u in range(STREAMS):
        a_copy(u).wait_send()
        for n in range(3):
            b_copy(u, n).wait_send()
        for d in range(1, nz):
            c_copy(u, d).wait_send()
            d_copy(u, d, z).wait_send()
        for n in range(1, 3):
            e_copy(u, n, True).wait_recv()
        for n in range(3):
            e_copy(u, n).wait_send()


def finish(scale, cr_in, re_in, ctx_out, grad_out, cr, re, sem):
    copies = [pltpu.make_async_copy(*pair, sem.at[n]) for n, pair in enumerate(((cr_in, cr), (re_in, re)))]
    for copy in copies:
        copy.start()
    copies[0].wait()
    for h in range(cr.shape[0]):
        ctx_out[:, h * HEAD : (h + 1) * HEAD] = cr[h, :, 0:HEAD]
    copies[1].wait()
    lanes = GROUP // STREAMS
    width = grad_out.shape[1]
    for u in range(STREAMS):
        for g in range(4):
            lo = g * GROUP + u * lanes
            hi = min(lo + lanes, width)
            block = re[u, g // 2, g % 2].reshape(PAD, lanes)[:HEAD, : hi - lo]
            grad_out[:, lo:hi] = block.astype(F32) * scale


def body(nz, features, segment_ids, projections, cotangent):
    ns = lax.axis_size("seq")
    ny = ns // 2
    width = features.shape[2]
    feat = features.reshape(2, HALF, width)
    seg = segment_ids.reshape(ns, ROWS)
    vmem = lambda *shape: pltpu.VMEM(shape, BF16)
    dma = lambda *shape: pltpu.SemaphoreType.DMA(shape)
    rows = 8 // nz
    lanes = GROUP // STREAMS
    reach = 2 * REACH + 1
    held = pl.BlockSpec(memory_space=pltpu.VMEM)
    far = pl.BlockSpec(memory_space=pltpu.HBM)
    kept = pl.BlockSpec(memory_space=pl.ANY)
    cr, re = pl.pallas_call(
        functools.partial(kernel, nz),
        out_shape=(
            jax.ShapeDtypeStruct((ns, ROWS, PAD), BF16),
            jax.ShapeDtypeStruct((STREAMS, 2, 2, 8, 16, lanes), BF16),
        ),
        in_specs=[far, far, far, held],
        out_specs=[held, held],
        scratch_shapes=[
            vmem(ny, 2, HALF, width),
            vmem(3, HEAD, width),
            vmem(2, 3, 2, 2, HALF // 2, width),
            vmem(ROWS, width),
            vmem(ns, ROWS, PAD),
            vmem(ns, ROWS, PAD),
            vmem(ns, 3, ROWS, PAD),
            vmem(ny, 3, ROWS, PAD),
            pltpu.VMEM((ns, ROWS, ROWS), F32),
            vmem(ny, reach, 2 * ROWS, 2 * ROWS),
            pltpu.VMEM((ny, 2 * ROWS, PAD), F32),
            pltpu.VMEM((ny, PAD, 2 * ROWS), F32),
            vmem(ns, ROWS, PAD),
            vmem(2, ny, PAD, ROWS),
            vmem(ny, PAD, ROWS),
            vmem(STREAMS, 2, 2, 2, 8, 16, lanes),
            vmem(STREAMS, 2, 2, 8, 16, lanes),
            vmem(STREAMS, 2, 2, 8, 16, lanes),
            vmem(STREAMS, 3, 8, 16, lanes),
            vmem(STREAMS, 8, 16, lanes),
            vmem(STREAMS, nz, rows, 16, lanes),
            vmem(STREAMS, rows, 16, lanes),
            dma(2, ny - 1), dma(2, ny - 1),
            dma(3),
            dma(3), dma(3), dma(3), dma(3), dma(2, 3), dma(2, 3),
            dma(ny), dma(ny),
            dma(ns), dma(ns),
            dma(ns), dma(ns),
            dma(ny), dma(ny),
            dma(STREAMS), dma(STREAMS),
            dma(STREAMS, 3), dma(STREAMS, 3),
            dma(STREAMS, nz), dma(STREAMS, nz),
            dma(STREAMS, nz), dma(STREAMS, nz),
            dma(STREAMS, 3), dma(STREAMS, 3),
        ],
        compiler_params=pltpu.CompilerParams(
            collective_id=0, has_side_effects=True, vmem_limit_bytes=62 * 1024 * 1024
        ),
    )(feat, projections, cotangent[0], seg)
    ctx, grad = pl.pallas_call(
        functools.partial(finish, 1.0 / (4 * nz)),
        out_shape=(
            jax.ShapeDtypeStruct((ROWS, width), BF16),
            jax.ShapeDtypeStruct((HEAD, width), F32),
        ),
        in_specs=[kept, kept],
        out_specs=[held, held],
        scratch_shapes=[
            vmem(ns, ROWS, PAD),
            vmem(STREAMS, 2, 2, 8, 16, lanes),
            dma(2),
        ],
    )(cr, re)
    return (ctx[None], grad)


def solution(mesh):
    in_specs = (P("dp", "seq", None), P("dp", None), P(None, "seq", None), P("dp", "seq", None))
    out_specs = (P("dp", "seq", None), P("seq", None))
    step = functools.partial(body, mesh.shape["dp"] // 4)
    return jax.shard_map(step, mesh=mesh, in_specs=in_specs, out_specs=out_specs, check_vma=False)
```

```python
import functools

import jax
import jax.numpy as jnp
from jax import lax
from jax.experimental import pallas as pl
from jax.experimental.pallas import tpu as pltpu
from jax.sharding import PartitionSpec as P

HEAD = 120
PAD = 128
ROWS = 128
HALF = 64
REACH = 2
STREAMS = 2
GROUP = 512
LOG2E = 1.4426950408889634
MESH = pl.DeviceIdType.MESH
NT = (((1,), (1,)), ((), ()))
NN = (((1,), (0,)), ((), ()))
TN = (((0,), (0,)), ((), ()))
F32 = jnp.float32
BF16 = jnp.bfloat16


def kernel(
    nz, feat, w, cot, seg, ctx_out, re_out,
    G, WR, WA, CO, CT, XO, DO, QKV, QS, SEGC, EB, INV, VRT, CP, XC, CR, CF,
    AB, AS, PB, RA, PA, RB, PC, RC, PD, RE,
    ring_s, ring_r, loc, w_s, w_r, wz_s, wz_r, wc_s, wc_r, qs_s, qs_r, dx_s, dx_r, do_s, do_r,
    xc_s, xc_r, cx_s, cx_r, vr_s, vr_r, a_s, a_r, b_s, b_r, c_s, c_r, d_s, d_r, e_s, e_r,
):
    ny = G.shape[0]
    ns = 2 * ny
    width = feat.shape[2]
    dp, sq = lax.axis_index("dp"), lax.axis_index("seq")
    core = lax.rem(dp, 2)
    xhi = lax.rem(lax.div(dp, 2), 2)
    z = lax.div(dp, 4)
    zlo = lax.rem(z, 2)
    y = lax.div(sq, 2)
    xlo = lax.rem(sq, 2)
    other = 1 - core
    peer_x = sq + 1 - 2 * xlo
    peer_core = dp + 1 - 2 * core
    peer_xhi = dp + 2 - 4 * xhi
    peer_z = dp + 4 - 8 * zlo

    def remote(src, dst, ssem, rsem, dev):
        return pltpu.make_async_remote_copy(
            src_ref=src, dst_ref=dst, send_sem=ssem, recv_sem=rsem, device_id=dev, device_id_type=MESH
        )

    own_feat = pltpu.make_async_copy(feat, G.at[y], loc.at[0])
    own_w = pltpu.make_async_copy(w, WR, loc.at[1])
    own_cot = pltpu.make_async_copy(cot, CO, loc.at[2])
    own_feat.start()
    own_w.start()
    own_cot.start()

    barrier = pltpu.get_barrier_semaphore()

    def hello(dev):
        pl.semaphore_signal(barrier, inc=1, device_id=dev, device_id_type=MESH)

    def hello_seq(d, carry):
        hello((dp, lax.rem(sq + d, ns)))
        return carry

    lax.fori_loop(1, ns, hello_seq, 0)
    hello((peer_core, sq))
    hello((peer_xhi, sq))
    hello((peer_xhi, peer_x))

    def z_dev(d):
        return lax.rem(z + d, nz) * 4 + lax.rem(dp, 4)

    def hello_z(d, carry):
        hello((z_dev(d), sq))
        return carry

    lax.fori_loop(1, nz, hello_z, 0)

    own_w.wait()
    quarter = HALF // 2
    for p in range(3):
        for c in range(4):
            lo = c * quarter
            hi = min(lo + quarter, HEAD)
            WA[0, p, c // 2, c % 2, 0 : hi - lo] = WR[p, lo:hi]
            if hi - lo < quarter:
                WA[0, p, c // 2, c % 2, hi - lo :] = jnp.zeros((quarter - hi + lo, width), BF16)
    own_feat.wait()
    pl.semaphore_wait(barrier, ns - 1 + 3 + nz - 1)

    last = ny - 1

    def ring(dirn, k, at):
        hops = k // 2
        if dirn == 0:
            shard, half, to = lax.rem(at + ny - hops, ny), k % 2, lax.rem(sq + 2, ns)
        else:
            shard, half, to = lax.rem(at + hops, ny), 1 - k % 2, lax.rem(sq + ns - 2, ns)
        ref = G.at[shard, half]
        return remote(ref, ref, ring_s.at[dirn, k], ring_r.at[dirn, k], (dp, to))

    def ring_send(dirn, k):
        return ring(dirn, k, y)

    def ring_recv(dirn, k):
        return ring(dirn, k, lax.rem(y + ny - 1, ny) if dirn == 0 else lax.rem(y + 1, ny))

    for k in range(2):
        for dirn in range(2):
            ring_send(dirn, k).start()

    def w_x(p):
        return remote(
            WA.at[0, p, core, zlo], WA.at[1, p, core, zlo], w_s.at[p], w_r.at[p], (dp, peer_x)
        )

    def w_z(p, at):
        ref = WA.at[1, p, core, at]
        return remote(ref, ref, wz_s.at[p], wz_r.at[p], (peer_z, sq))

    def w_c(p, c, at, n):
        ref = WA.at[1, p, c, at]
        return remote(ref, ref, wc_s.at[n, p], wc_r.at[n, p], (peer_core, sq))

    for p in range(3):
        w_x(p).start()

    own_cot.wait()
    for r in range(ny):
        left = CO[:, 2 * r * HEAD : (2 * r + 1) * HEAD]
        right = CO[:, (2 * r + 1) * HEAD : (2 * r + 2) * HEAD]
        XO[r] = jnp.zeros((ROWS, PAD), BF16)
        XO[r, :, 0:HEAD] = jnp.where(xlo == 0, right, left)
        CT[r, xlo] = jnp.zeros((ROWS, PAD), BF16)
        CT[r, xlo, :, 0:HEAD] = jnp.where(xlo == 0, left, right)

    def dx_copy(col):
        return remote(XO, CT.at[:, col], dx_s, dx_r, (dp, peer_x))

    dx_copy(xlo).start()

    def label_col(b, carry):
        row = seg[pl.ds(b, 1), :].astype(F32)
        SEGC[b] = jnp.broadcast_to(row, (ROWS, ROWS)).T
        return carry

    lax.fori_loop(0, ns, label_col, 0)
    VRT[...] = jnp.zeros_like(VRT)

    def at_y(d):
        return lax.rem(y + d + ny, ny)

    def arrive(k):
        for dirn in range(2):
            ring_recv(dirn, k).wait_recv()
            if k + 2 <= last - 1:
                ring_send(dirn, k + 2).start()

    for p in range(3):
        w_x(p).wait_recv()
        w_z(p, zlo).start()
        w_c(p, core, zlo, 0).start()
    arrive(0)
    for p in range(3):
        w_z(p, 1 - zlo).wait_recv()
        w_c(p, core, 1 - zlo, 1).start()
    arrive(1)

    def qs_copy(shard):
        return remote(
            QS.at[shard], QKV.at[2 * shard + xlo], qs_s.at[shard], qs_r.at[shard], (dp, peer_x)
        )

    def project(shard, apart=False):
        x = G[shard].reshape(ROWS, width)

        def heads(wall):
            wall = wall.reshape(-1, width)
            return lax.dot_general(x, wall, NT, preferred_element_type=F32).astype(BF16)

        if apart:
            near, far = heads(WA[0]), heads(WA[1])
        else:
            both = heads(WA[...])
            near, far = both[:, : 3 * PAD], both[:, 3 * PAD :]
        for p in range(3):
            QS[shard, p] = far[:, p * PAD : (p + 1) * PAD]
        qs_copy(shard).start()
        for p in range(3):
            QKV[2 * shard + xlo, p] = near[:, p * PAD : (p + 1) * PAD]

    def qs_wait(shard):
        b = 2 * shard + (1 - xlo)
        remote(
            QS.at[shard], QKV.at[b], qs_s.at[shard], qs_r.at[shard], (dp, peer_x)
        ).wait_recv()

    def do_copy(r):
        return remote(CT.at[r], DO.at[y], do_s.at[r], do_r.at[y], (dp, 2 * r + xlo))

    scale = HEAD ** (-0.5) * LOG2E

    def rows_of(p, r):
        return QKV[pl.ds(2 * r, 2), p].reshape(2 * ROWS, PAD)

    def attend(i):
        q = rows_of(0, i)
        col = SEGC[pl.ds(2 * i, 2)].reshape(2 * ROWS, PAD)
        parts = []
        for o in range(-REACH, REACH + 1):
            r = lax.rem(i + o + ny, ny)
            s = lax.dot_general(q, rows_of(1, r), NT, preferred_element_type=F32)
            for c in range(2):
                row = seg[pl.ds(2 * r + c, 1), :].astype(F32)
                parts.append(jnp.where(col == row, s[:, c * PAD : (c + 1) * PAD], -1e30))
        top = functools.reduce(jnp.maximum, parts)
        top = jnp.max(top, axis=1, keepdims=True)
        total = jnp.zeros((2 * ROWS, PAD), F32)
        ctx = jnp.zeros((2 * ROWS, PAD), F32)
        for n in range(2 * REACH + 1):
            left, right = (jnp.exp2((part - top) * scale) for part in parts[2 * n : 2 * n + 2])
            total += left + right
            e = jnp.concatenate([left.astype(BF16), right.astype(BF16)], axis=1)
            EB[i, n] = e
            r = lax.rem(i + n - REACH + ny, ny)
            ctx += lax.dot_general(e, rows_of(2, r), NN, preferred_element_type=F32)
        inv = jnp.broadcast_to(1.0 / jnp.sum(total, axis=1, keepdims=True), (2 * ROWS, PAD))
        INV[i] = inv
        ctx = (ctx * inv).astype(BF16)
        left, right = ctx[:ROWS], ctx[ROWS:]
        XC[i] = jnp.where(xlo == 0, right, left)
        xc_copy(i, xlo).start()
        CP[i, xlo] = jnp.where(xlo == 0, left, right)

    def xc_copy(i, head):
        return remote(XC.at[i], CP.at[i, head], xc_s.at[i], xc_r.at[i], (dp, peer_x))

    def attend_at(d, carry):
        attend(at_y(d))
        return carry

    arrive(2)
    for p in range(3):
        w_c(p, other, zlo, 0).wait_recv()
        w_c(p, other, 1 - zlo, 1).wait_recv()
    project(y)
    arrive(3)
    project(at_y(1))
    project(at_y(-1))
    arrive(4)
    dx_copy(1 - xlo).wait_recv()
    for d in (4, 3, -3):
        do_copy(at_y(d)).start()
    DO[y] = CT[y]
    project(at_y(2))
    project(at_y(-2))
    arrive(5)
    for d in (2, -2, 1, -1):
        do_copy(at_y(d)).start()
    project(at_y(3))
    project(at_y(-3))
    for d in (0, 1, -1, 2, -2):
        qs_wait(at_y(d))
    attend(y)
    arrive(6)
    project(at_y(4), apart=True)
    qs_wait(at_y(3))
    qs_wait(at_y(-3))
    lax.fori_loop(0, 2, lambda t, carry: attend_at(1 + 6 * t, carry), 0)
    qs_wait(at_y(4))
    lax.fori_loop(2, ny - 1, attend_at, 0)

    def vr_copy(r):
        return remote(AS.at[r], AB.at[1, r], vr_s.at[r], vr_r.at[r], (dp, peer_x))

    def value_rows_out(r):
        v = VRT[r].astype(BF16)
        left, right = v[:, :PAD], v[:, PAD:]
        AS[r] = jnp.where(xlo == 0, right, left)
        vr_copy(r).start()
        AB[0, r] = jnp.where(xlo == 0, left, right)

    def value_step(t, carry):
        i = lax.rem(y + 4 + t, ny)

        @pl.when(i != y)
        def _():
            remote(CT.at[i], DO.at[i], do_s.at[i], do_r.at[i], (dp, 2 * i + xlo)).wait_recv()

        up = DO[i].reshape(2 * ROWS, PAD).astype(F32) * INV[i]
        up = up.astype(BF16)
        for n in range(2 * REACH + 1):
            r = lax.rem(i + n - REACH + ny, ny)
            VRT[r] += lax.dot_general(up, EB[i, n], TN, preferred_element_type=F32)

        @pl.when(t >= 4)
        def _():
            value_rows_out(lax.rem(y + 2 + t, ny))

        return carry

    lax.fori_loop(0, ny, value_step, 0)
    for d in range(2, 6):
        value_rows_out(at_y(d))

    def cx_copy(r):
        return remote(CP.at[r], CR.at[y], cx_s.at[r], cx_r.at[y], (dp, 2 * r + xlo))

    for d in (4, 3, -3, 2, -2, 1, -1):
        xc_copy(at_y(d), 1 - xlo).wait_recv()
        cx_copy(at_y(d)).start()
    xc_copy(y, 1 - xlo).wait_recv()
    CR[y] = CP[y]

    lanes = GROUP // STREAMS

    def a_copy(u, h):
        return remote(PB.at[u, other, h], RA.at[u, h], a_s.at[u, h], a_r.at[u, h], (peer_core, sq))

    def product(h):
        lhs = jnp.concatenate([AB[h, t] for t in range(ny)], axis=1)
        for u in range(STREAMS):
            for g in range(4):
                lo = (4 * u + g) * lanes
                hi = min(lo + lanes, width)
                rhs = G[:, :, :, lo:hi].reshape(ny * ROWS, hi - lo)
                part = lax.dot_general(lhs, rhs, NN, preferred_element_type=F32).astype(BF16)
                if hi - lo < lanes:
                    part = jnp.concatenate([part, jnp.zeros((PAD, lanes - hi + lo), BF16)], axis=1)
                PB[u, g % 2, h, g // 2] = part.reshape(8, 16, lanes)
            a_copy(u, h).start()

    def b_copy(u, n):
        h, g = (1, xhi) if n == 0 else (0, 1 - xhi) if n == 1 else (1, 1 - xhi)
        dev = (dp if n == 0 else peer_xhi, sq if n == 1 else peer_x)
        return remote(PA.at[u, h, g], RB.at[u, n], b_s.at[u, n], b_r.at[u, n], dev)

    def core_sum(u, h):
        a_copy(u, h).wait_recv()
        for g in range(2):
            PA[u, h, g] = (PB[u, core, h, g].astype(F32) + RA[u, h, g].astype(F32)).astype(BF16)

    product(0)
    for u in range(STREAMS):
        core_sum(u, 0)
        b_copy(u, 1).start()
    for r in range(ny):
        vr_copy(r).wait_recv()
    product(1)
    for u in range(STREAMS):
        core_sum(u, 1)
        b_copy(u, 2).start()
        b_copy(u, 0).start()

    rows = 8 // nz

    def c_copy(u, d):
        to = lax.rem(z + d, nz)
        return remote(
            PC.at[u, pl.ds(to * rows, rows)], RC.at[u, d], c_s.at[u, d], c_r.at[u, d], (z_dev(d), sq)
        )

    by_reach = sorted(range(1, nz), key=lambda d: -min(d, nz - d))
    for u in range(STREAMS):
        total = PA[u, 0, xhi].astype(F32)
        for n in (1, 0, 2):
            b_copy(u, n).wait_recv()
            total += RB[u, n].astype(F32)
        PC[u] = total.astype(BF16)
        for d in by_reach:
            c_copy(u, d).start()

    def d_copy(u, d, frm):
        return remote(
            PD.at[u],
            RE.at[u, xhi, core, pl.ds(frm * rows, rows)],
            d_s.at[u, d],
            d_r.at[u, d],
            (z_dev(d), sq),
        )

    for u in range(STREAMS):
        total = PC[u, pl.ds(z * rows, rows)].astype(F32)
        for d in range(1, nz):
            c_copy(u, d).wait_recv()
            total += RC[u, d].astype(F32)
        PD[u] = total.astype(BF16)
        for d in by_reach:
            d_copy(u, d, z).start()
        RE[u, xhi, core, pl.ds(z * rows, rows)] = total.astype(BF16)

    def e_copy(u, n, recv=False):
        c = other if recv and n > 0 else core
        hi = 1 - xhi if (n == 2) != (recv and n == 0) else xhi
        ref = RE.at[u, hi, c]
        dev = (peer_xhi if n == 0 else peer_core, sq)
        return remote(ref, ref, e_s.at[u, n], e_r.at[u, n], dev)

    for d in range(1, ny):
        r = at_y(d)
        remote(CP.at[r], CR.at[r], cx_s.at[r], cx_r.at[r], (dp, 2 * r + xlo)).wait_recv()
    for h in range(ns):
        CF[:, h * HEAD : (h + 1) * HEAD] = CR[h // 2, h % 2, :, 0:HEAD]
    ctx_copy = pltpu.make_async_copy(CF, ctx_out, loc.at[0])
    ctx_copy.start()

    for u in range(STREAMS):
        for d in range(1, nz):
            d_copy(u, d, lax.rem(z + nz - d, nz)).wait_recv()
        e_copy(u, 0).start()
        e_copy(u, 1).start()
    for u in range(STREAMS):
        e_copy(u, 0, True).wait_recv()
        e_copy(u, 2).start()
    re_copies = [pltpu.make_async_copy(RE.at[u], re_out.at[u], loc.at[1 + u]) for u in range(STREAMS)]
    for u in range(STREAMS):
        for n in range(1, 3):
            e_copy(u, n, True).wait_recv()
        re_copies[u].start()

    for k in range(last):
        for dirn in range(2):
            ring_send(dirn, k).wait_send()
    for p in range(3):
        w_x(p).wait_send()
        w_z(p, zlo).wait_send()
        w_c(p, core, zlo, 0).wait_send()
        w_c(p, core, 1 - zlo, 1).wait_send()
    dx_copy(xlo).wait_send()
    for r in range(ny):
        qs_copy(r).wait_send()
        xc_copy(r, xlo).wait_send()
        vr_copy(r).wait_send()
    for d in range(1, ny):
        do_copy(at_y(d)).wait_send()
        cx_copy(at_y(d)).wait_send()
    for u in range(STREAMS):
        for h in range(2):
            a_copy(u, h).wait_send()
        for n in range(3):
            b_copy(u, n).wait_send()
            e_copy(u, n).wait_send()
        for d in range(1, nz):
            c_copy(u, d).wait_send()
            d_copy(u, d, z).wait_send()
    ctx_copy.wait()
    for copy in re_copies:
        copy.wait()


def finish(scale, ctx_in, re_in, ctx_out, grad_out, ctx, re, grad, sem):
    lanes = GROUP // STREAMS
    width = grad_out.shape[1]
    halves = [(4 * lanes * u, min(4 * lanes * (u + 1), width)) for u in range(STREAMS)]
    parts = [pltpu.make_async_copy(re_in.at[u], re.at[u], sem.at[u]) for u in range(STREAMS)]
    ctx_read = pltpu.make_async_copy(ctx_in, ctx, sem.at[STREAMS])
    ctx_write = pltpu.make_async_copy(ctx, ctx_out, sem.at[STREAMS])
    writes = [
        pltpu.make_async_copy(grad.at[:, lo:hi], grad_out.at[:, lo:hi], sem.at[u])
        for u, (lo, hi) in enumerate(halves)
    ]
    for copy in (*parts, ctx_read):
        copy.start()
    for u in range(STREAMS):
        parts[u].wait()
        for g in range(4):
            lo = (4 * u + g) * lanes
            hi = min(lo + lanes, width)
            block = re[u, g // 2, g % 2].reshape(PAD, lanes)[:HEAD, : hi - lo]
            grad[:, lo:hi] = block.astype(F32) * scale
        writes[u].start()
        if u == 0:
            ctx_read.wait()
            ctx_write.start()
    for copy in (*writes, ctx_write):
        copy.wait()


def body(nz, features, segment_ids, projections, cotangent):
    ns = lax.axis_size("seq")
    ny = ns // 2
    width = features.shape[2]
    feat = features.reshape(2, HALF, width)
    seg = segment_ids.reshape(ns, ROWS)
    vmem = lambda *shape: pltpu.VMEM(shape, BF16)
    dma = lambda *shape: pltpu.SemaphoreType.DMA(shape)
    rows = 8 // nz
    lanes = GROUP // STREAMS
    reach = 2 * REACH + 1
    held = pl.BlockSpec(memory_space=pltpu.VMEM)
    far = pl.BlockSpec(memory_space=pltpu.HBM)
    ctx, re = pl.pallas_call(
        functools.partial(kernel, nz),
        out_shape=(
            jax.ShapeDtypeStruct((ROWS, width), BF16),
            jax.ShapeDtypeStruct((STREAMS, 2, 2, 8, 16, lanes), BF16),
        ),
        in_specs=[far, far, far, held],
        out_specs=[far, far],
        scratch_shapes=[
            vmem(ny, 2, HALF, width),
            vmem(3, HEAD, width),
            vmem(2, 3, 2, 2, HALF // 2, width),
            vmem(ROWS, width),
            vmem(ny, 2, ROWS, PAD),
            vmem(ny, ROWS, PAD),
            vmem(ny, 2, ROWS, PAD),
            vmem(ns, 3, ROWS, PAD),
            vmem(ny, 3, ROWS, PAD),
            pltpu.VMEM((ns, ROWS, ROWS), F32),
            vmem(ny, reach, 2 * ROWS, 2 * ROWS),
            pltpu.VMEM((ny, 2 * ROWS, PAD), F32),
            pltpu.VMEM((ny, PAD, 2 * ROWS), F32),
            vmem(ny, 2, ROWS, PAD),
            vmem(ny, ROWS, PAD),
            vmem(ny, 2, ROWS, PAD),
            vmem(ROWS, width),
            vmem(2, ny, PAD, ROWS),
            vmem(ny, PAD, ROWS),
            vmem(STREAMS, 2, 2, 2, 8, 16, lanes),
            vmem(STREAMS, 2, 2, 8, 16, lanes),
            vmem(STREAMS, 2, 2, 8, 16, lanes),
            vmem(STREAMS, 3, 8, 16, lanes),
            vmem(STREAMS, 8, 16, lanes),
            vmem(STREAMS, nz, rows, 16, lanes),
            vmem(STREAMS, rows, 16, lanes),
            vmem(STREAMS, 2, 2, 8, 16, lanes),
            dma(2, ny - 1), dma(2, ny - 1),
            dma(3),
            dma(3), dma(3), dma(3), dma(3), dma(2, 3), dma(2, 3),
            dma(ny), dma(ny),
            dma(), dma(),
            dma(ny), dma(ny),
            dma(ny), dma(ny),
            dma(ny), dma(ny),
            dma(ny), dma(ny),
            dma(STREAMS, 2), dma(STREAMS, 2),
            dma(STREAMS, 3), dma(STREAMS, 3),
            dma(STREAMS, nz), dma(STREAMS, nz),
            dma(STREAMS, nz), dma(STREAMS, nz),
            dma(STREAMS, 3), dma(STREAMS, 3),
        ],
        compiler_params=pltpu.CompilerParams(
            collective_id=0, has_side_effects=True, vmem_limit_bytes=62 * 1024 * 1024
        ),
    )(feat, projections, cotangent[0], seg)
    ctx, grad = pl.pallas_call(
        functools.partial(finish, 1.0 / (4 * nz)),
        out_shape=(
            jax.ShapeDtypeStruct((ROWS, width), BF16),
            jax.ShapeDtypeStruct((HEAD, width), F32),
        ),
        in_specs=[far, far],
        out_specs=[far, far],
        scratch_shapes=[
            vmem(ROWS, width),
            vmem(STREAMS, 2, 2, 8, 16, lanes),
            pltpu.VMEM((HEAD, width), F32),
            dma(STREAMS + 1),
        ],
    )(ctx, re)
    return (ctx[None], grad)


def solution(mesh):
    in_specs = (P("dp", "seq", None), P("dp", None), P(None, "seq", None), P("dp", "seq", None))
    out_specs = (P("dp", "seq", None), P("seq", None))
    step = functools.partial(body, mesh.shape["dp"] // 4)
    return jax.shard_map(step, mesh=mesh, in_specs=in_specs, out_specs=out_specs, check_vma=False)
```

```python
import functools

import jax
import jax.numpy as jnp
from jax import lax
from jax.experimental import pallas as pl
from jax.experimental.pallas import tpu as pltpu
from jax.sharding import PartitionSpec as P

HEAD = 120
PAD = 128
ROWS = 128
HALF = 64
REACH = 2
STREAMS = 4
GROUP = 512
RING, WALL, DX, QSENT, DSENT, XSENT, VSENT, CSENT, ASENT, BSENT, ZSENT, TSENT, ESENT = range(13)
LOG2E = 1.4426950408889634
MESH = pl.DeviceIdType.MESH
NT = (((1,), (1,)), ((), ()))
NN = (((1,), (0,)), ((), ()))
TN = (((0,), (0,)), ((), ()))
F32 = jnp.float32
BF16 = jnp.bfloat16


def kernel(
    nz, feat, w, cot, seg_in, ctx_out, re_out,
    seg, G, WR, WA, CO, CT, XO, DO, QKV, QS, SEGC, EB, INV, VRT, CP, XC, CR, CF,
    AB, AS, PB, RA, PA, RB, PC, RC, PD, RE,
    sent, ring_r, loc, w_r, wz_r, wc_r, qs_r, dx_r, do_r, xc_r, cx_r, vr_r, a_r, b_r, c_r, d_r, e_r,
):
    ny = G.shape[0]
    ns = 2 * ny
    width = feat.shape[2]
    dp, sq = lax.axis_index("dp"), lax.axis_index("seq")
    core = lax.rem(dp, 2)
    xhi = lax.rem(lax.div(dp, 2), 2)
    z = lax.div(dp, 4)
    zlo = lax.rem(z, 2)
    y = lax.div(sq, 2)
    xlo = lax.rem(sq, 2)
    other = 1 - core
    peer_x = sq + 1 - 2 * xlo
    peer_core = dp + 1 - 2 * core
    peer_xhi = dp + 2 - 4 * xhi
    peer_z = dp + 4 - 8 * zlo

    def remote(src, dst, kind, rsem, dev):
        return pltpu.make_async_remote_copy(
            src_ref=src,
            dst_ref=dst,
            send_sem=sent.at[kind],
            recv_sem=rsem,
            device_id=dev,
            device_id_type=MESH,
        )

    def landed(ref, sem):
        pltpu.make_async_copy(ref, ref, sem).wait()

    own_feat = pltpu.make_async_copy(feat, G.at[y], loc.at[0])
    own_w = pltpu.make_async_copy(w, WR, loc.at[1])
    own_cot = pltpu.make_async_copy(cot, CO, loc.at[2])
    own_seg = pltpu.make_async_copy(seg_in, seg, loc.at[3])
    for copy in (own_feat, own_w, own_cot, own_seg):
        copy.start()

    barrier = pltpu.get_barrier_semaphore()

    def hello(dev):
        pl.semaphore_signal(barrier, inc=1, device_id=dev, device_id_type=MESH)

    def hello_seq(d, carry):
        hello((dp, lax.rem(sq + d, ns)))
        return carry

    lax.fori_loop(1, ns, hello_seq, 0)
    hello((peer_core, sq))
    hello((peer_xhi, sq))
    hello((peer_xhi, peer_x))

    def z_dev(d):
        return lax.rem(z + d, nz) * 4 + lax.rem(dp, 4)

    def hello_z(d, carry):
        hello((z_dev(d), sq))
        return carry

    lax.fori_loop(1, nz, hello_z, 0)

    own_feat.wait()
    pl.semaphore_wait(barrier, ns - 1 + 3 + nz - 1)

    last = ny - 1

    def ring(dirn, k, at):
        hops = k // 2
        if dirn == 0:
            shard, half, to = lax.rem(at + ny - hops, ny), k % 2, lax.rem(sq + 2, ns)
        else:
            shard, half, to = lax.rem(at + hops, ny), 1 - k % 2, lax.rem(sq + ns - 2, ns)
        ref = G.at[shard, half]
        return remote(ref, ref, RING, ring_r.at[dirn, k], (dp, to))

    def ring_send(dirn, k):
        return ring(dirn, k, y)

    def ring_recv(dirn, k):
        return ring(dirn, k, lax.rem(y + ny - 1, ny) if dirn == 0 else lax.rem(y + 1, ny))

    for k in range(2):
        for dirn in range(2):
            ring_send(dirn, k).start()

    own_w.wait()
    quarter = HALF // 2
    for p in range(3):
        for c in range(4):
            lo = c * quarter
            hi = min(lo + quarter, HEAD)
            WA[0, p, c // 2, c % 2, 0 : hi - lo] = WR[p, lo:hi]
            if hi - lo < quarter:
                WA[0, p, c // 2, c % 2, hi - lo :] = jnp.zeros((quarter - hi + lo, width), BF16)
    def w_x(p):
        return remote(
            WA.at[0, p, core, zlo], WA.at[1, p, core, zlo], WALL, w_r.at[p], (dp, peer_x)
        )

    def w_z(p, at):
        ref = WA.at[1, p, core, at]
        return remote(ref, ref, WALL, wz_r.at[p], (peer_z, sq))

    def w_c(p, at):
        ref = WA.at[1, p, core, at]
        return remote(ref, ref, WALL, wc_r, (peer_core, sq))

    for p in range(3):
        w_x(p).start()

    own_cot.wait()
    for r in range(ny):
        left = CO[:, 2 * r * HEAD : (2 * r + 1) * HEAD]
        right = CO[:, (2 * r + 1) * HEAD : (2 * r + 2) * HEAD]
        XO[r] = jnp.zeros((ROWS, PAD), BF16)
        XO[r, :, 0:HEAD] = jnp.where(xlo == 0, right, left)
        CT[r, xlo] = jnp.zeros((ROWS, PAD), BF16)
        CT[r, xlo, :, 0:HEAD] = jnp.where(xlo == 0, left, right)

    def dx_copy(col):
        return remote(XO, CT.at[:, col], DX, dx_r, (dp, peer_x))

    dx_copy(xlo).start()

    def label_col(b, carry):
        row = seg[pl.ds(b, 1), :].astype(F32)
        SEGC[b] = jnp.broadcast_to(row, (ROWS, ROWS)).T
        return carry

    own_seg.wait()
    lax.fori_loop(0, ns, label_col, 0)
    VRT[...] = jnp.zeros_like(VRT)

    def at_y(d):
        return lax.rem(y + d + ny, ny)

    def arrive(k):
        for dirn in range(2):
            ring_recv(dirn, k).wait_recv()
            if k + 2 <= last - 1:
                ring_send(dirn, k + 2).start()

    for p in range(3):
        w_x(p).wait_recv()
        w_z(p, zlo).start()
        w_c(p, zlo).start()
    arrive(0)
    for p in range(3):
        w_z(p, 1 - zlo).wait_recv()
        w_c(p, 1 - zlo).start()
    arrive(1)

    def qs_copy(d):
        shard = at_y(d)
        n = 0 if abs(d) < 3 else abs(d) - 2
        return remote(QS.at[shard], QKV.at[2 * shard + xlo], QSENT, qs_r.at[n], (dp, peer_x))

    def project(d, apart=False):
        shard = at_y(d)
        x = G[shard].reshape(ROWS, width)

        def heads(wall):
            wall = wall.reshape(-1, width)
            return lax.dot_general(x, wall, NT, preferred_element_type=F32).astype(BF16)

        if apart:
            near, far = heads(WA[0]), heads(WA[1])
        else:
            both = heads(WA[...])
            near, far = both[:, : 3 * PAD], both[:, 3 * PAD :]
        for p in range(3):
            QS[shard, p] = far[:, p * PAD : (p + 1) * PAD]
        qs_copy(d).start()
        for p in range(3):
            QKV[2 * shard + xlo, p] = near[:, p * PAD : (p + 1) * PAD]

    def do_copy(d):
        r = at_y(d)
        n = 0 if abs(d) == 1 else (ny - d) % ny - 1
        return remote(CT.at[r], DO.at[y], DSENT, do_r.at[n], (dp, 2 * r + xlo))

    scale = HEAD ** (-0.5) * LOG2E

    def rows_of(p, r):
        return QKV[pl.ds(2 * r, 2), p].reshape(2 * ROWS, PAD)

    def attend(i):
        q = rows_of(0, i)
        col = SEGC[pl.ds(2 * i, 2)].reshape(2 * ROWS, PAD)
        parts = []
        for o in range(-REACH, REACH + 1):
            r = lax.rem(i + o + ny, ny)
            s = lax.dot_general(q, rows_of(1, r), NT, preferred_element_type=F32)
            for c in range(2):
                row = seg[pl.ds(2 * r + c, 1), :].astype(F32)
                parts.append(jnp.where(col == row, s[:, c * PAD : (c + 1) * PAD], -1e30))
        top = functools.reduce(jnp.maximum, parts)
        top = jnp.max(top, axis=1, keepdims=True)
        total = jnp.zeros((2 * ROWS, PAD), F32)
        ctx = jnp.zeros((2 * ROWS, PAD), F32)
        for n in range(2 * REACH + 1):
            left, right = (jnp.exp2((part - top) * scale) for part in parts[2 * n : 2 * n + 2])
            total += left + right
            e = jnp.concatenate([left.astype(BF16), right.astype(BF16)], axis=1)
            EB[i, n] = e
            r = lax.rem(i + n - REACH + ny, ny)
            ctx += lax.dot_general(e, rows_of(2, r), NN, preferred_element_type=F32)
        inv = jnp.broadcast_to(1.0 / jnp.sum(total, axis=1, keepdims=True), (2 * ROWS, PAD))
        INV[i] = inv
        ctx = (ctx * inv).astype(BF16)
        left, right = ctx[:ROWS], ctx[ROWS:]
        XC[i] = jnp.where(xlo == 0, right, left)
        xc_copy(i, xlo).start()
        CP[i, xlo] = jnp.where(xlo == 0, left, right)

    def xc_copy(i, head):
        return remote(XC.at[i], CP.at[i, head], XSENT, xc_r, (dp, peer_x))

    def attend_at(d, carry):
        attend(at_y(d))
        return carry

    arrive(2)
    landed(WA.at[1, :, other], wc_r)
    project(0)
    arrive(3)
    project(1)
    project(-1)
    arrive(4)
    dx_copy(1 - xlo).wait_recv()
    for d in (1, -1, 4, 3):
        do_copy(d).start()
    DO[y] = CT[y]
    project(2)
    project(-2)
    arrive(5)
    for d in (-3, 2, -2):
        do_copy(d).start()
    project(3)
    project(-3)
    landed(QS.at[pl.ds(0, 5)], qs_r.at[0])
    attend(y)
    arrive(6)
    project(4, apart=True)
    landed(QS.at[pl.ds(0, 2)], qs_r.at[1])
    lax.fori_loop(0, 2, lambda t, carry: attend_at(1 + 6 * t, carry), 0)

    def vr_copy(r):
        return remote(AS.at[r], AB.at[1, r], VSENT, vr_r, (dp, peer_x))

    def value_rows_out(r):
        v = VRT[r].astype(BF16)
        left, right = v[:, :PAD], v[:, PAD:]
        AS[r] = jnp.where(xlo == 0, right, left)
        vr_copy(r).start()
        AB[0, r] = jnp.where(xlo == 0, left, right)

    def value_step(i):
        up = DO[i].reshape(2 * ROWS, PAD).astype(F32) * INV[i]
        up = up.astype(BF16)
        for n in range(2 * REACH + 1):
            r = lax.rem(i + n - REACH + ny, ny)
            VRT[r] += lax.dot_general(up, EB[i, n], TN, preferred_element_type=F32)

    def value_at(d, carry):
        value_step(at_y(d))
        return carry

    value_step(y)
    landed(DO.at[pl.ds(0, 2)], do_r.at[0])
    lax.fori_loop(0, 2, lambda t, carry: value_at(1 + 6 * t, carry), 0)
    landed(QS.at[0], qs_r.at[2])

    def far_rows(d, carry):
        attend(at_y(d))

        @pl.when(d > 2)
        def _():
            landed(DO.at[at_y(d - 1)], do_r.at[d - 2])
            value_step(at_y(d - 1))

        @pl.when(d > 3)
        def _():
            value_rows_out(at_y(d - 3))

        return carry

    lax.fori_loop(2, ny - 1, far_rows, 0)
    landed(DO.at[at_y(-2)], do_r.at[ny - 3])
    value_step(at_y(-2))
    for d in (4, 5, 6, 7, 0):
        value_rows_out(at_y(d))

    def cx_copy(r):
        return remote(CP.at[r], CR.at[y], CSENT, cx_r, (dp, 2 * r + xlo))

    lanes = GROUP // STREAMS

    def a_copy(u, h):
        return remote(PB.at[u, other, h], RA.at[u, h], ASENT, a_r.at[u, h], (peer_core, sq))

    def product(h):
        lhs = jnp.concatenate([AB[h, t] for t in range(ny)], axis=1)
        for u in range(STREAMS):
            lo = 4 * u * lanes
            hi = min(lo + 4 * lanes, width)
            rhs = G[:, :, :, lo:hi].reshape(ny * ROWS, hi - lo)
            part = lax.dot_general(lhs, rhs, NN, preferred_element_type=F32).astype(BF16)
            if hi - lo < 4 * lanes:
                part = jnp.concatenate([part, jnp.zeros((PAD, 4 * lanes - hi + lo), BF16)], axis=1)
            for g in range(4):
                block = part[:, g * lanes : (g + 1) * lanes]
                PB[u, g % 2, h, g // 2] = block.reshape(8, 16, lanes)
            a_copy(u, h).start()

    def b_copy(u, n):
        h, g = (1, xhi) if n == 0 else (0, 1 - xhi) if n == 1 else (1, 1 - xhi)
        dev = (dp if n == 0 else peer_xhi, sq if n == 1 else peer_x)
        return remote(PA.at[u, h, g], RB.at[u, n], BSENT, b_r.at[u], dev)

    def core_sum(u, h):
        a_copy(u, h).wait_recv()
        for g in range(2):
            PA[u, h, g] = (PB[u, core, h, g].astype(F32) + RA[u, h, g].astype(F32)).astype(BF16)

    product(0)
    for u in range(STREAMS):
        core_sum(u, 0)
        b_copy(u, 1).start()
    landed(AS, vr_r)
    product(1)
    landed(XC, xc_r)
    for d in (4, 3, -3, 2, -2, 1, -1):
        cx_copy(at_y(d)).start()
    CR[y] = CP[y]
    for u in range(STREAMS):
        core_sum(u, 1)
        b_copy(u, 2).start()
        b_copy(u, 0).start()

    rows = 8 // nz

    def c_copy(u, d):
        to = lax.rem(z + d, nz)
        return remote(
            PC.at[u, pl.ds(to * rows, rows)], RC.at[u, d], ZSENT, c_r.at[u], (z_dev(d), sq)
        )

    by_reach = sorted(range(1, nz), key=lambda d: -min(d, nz - d))
    for u in range(STREAMS):
        total = PA[u, 0, xhi].astype(F32)
        landed(RB.at[u], b_r.at[u])
        for n in range(3):
            total += RB[u, n].astype(F32)
        PC[u] = total.astype(BF16)
        for d in by_reach:
            c_copy(u, d).start()

    def d_copy(u, d):
        into = RE.at[u, xhi, core, pl.ds(z * rows, rows)]
        return remote(PD.at[u], into, TSENT, d_r.at[u], (z_dev(d), sq))

    for u in range(STREAMS):
        total = PC[u, pl.ds(z * rows, rows)].astype(F32)
        landed(RC.at[u, pl.ds(1, nz - 1)], c_r.at[u])
        for d in range(1, nz):
            total += RC[u, d].astype(F32)
        PD[u] = total.astype(BF16)
        for d in by_reach:
            d_copy(u, d).start()
        RE[u, xhi, core, pl.ds(z * rows, rows)] = total.astype(BF16)

    def e_copy(u, n, recv=False):
        c = other if recv and n > 0 else core
        hi = 1 - xhi if (n == 2) != (recv and n == 0) else xhi
        ref = RE.at[u, hi, c]
        dev = (peer_xhi if n == 0 else peer_core, sq)
        return remote(ref, ref, ESENT, e_r.at[u, min(n, 1)], dev)

    landed(CR.at[pl.ds(0, ny - 1)], cx_r)
    for h in range(ns):
        CF[:, h * HEAD : (h + 1) * HEAD] = CR[h // 2, h % 2, :, 0:HEAD]
    ctx_copy = pltpu.make_async_copy(CF, ctx_out, loc.at[0])
    ctx_copy.start()

    for u in range(STREAMS):
        landed(RC.at[u, pl.ds(1, nz - 1)], d_r.at[u])
        e_copy(u, 0).start()
        e_copy(u, 1).start()
    for u in range(STREAMS):
        e_copy(u, 0, True).wait_recv()
        e_copy(u, 2).start()
    re_copies = [pltpu.make_async_copy(RE.at[u], re_out.at[u], loc.at[1 + u]) for u in range(STREAMS)]
    for u in range(STREAMS):
        landed(RE.at[u, :, other], e_r.at[u, 1])
        re_copies[u].start()

    for kind, ref in (
        (RING, G.at[pl.ds(0, last)]),
        (WALL, WA.at[1]),
        (DX, XO),
        (QSENT, QS),
        (DSENT, CT.at[pl.ds(0, ny - 1)]),
        (XSENT, XC),
        (VSENT, AS),
        (CSENT, CP.at[pl.ds(0, ny - 1)]),
        (ASENT, RA),
        (BSENT, RB),
        (ZSENT, RC.at[:, pl.ds(1, nz - 1)]),
        (TSENT, RC.at[:, pl.ds(1, nz - 1)]),
        (ESENT, RB),
    ):
        landed(ref, sent.at[kind])
    ctx_copy.wait()
    for copy in re_copies:
        copy.wait()


def finish(scale, ctx_in, re_in, ctx_out, grad_out, ctx, re, grad, sem):
    lanes = GROUP // STREAMS
    width = grad_out.shape[1]
    halves = [(4 * lanes * u, min(4 * lanes * (u + 1), width)) for u in range(STREAMS)]
    parts = [pltpu.make_async_copy(re_in.at[u], re.at[u], sem.at[u]) for u in range(STREAMS)]
    ctx_read = pltpu.make_async_copy(ctx_in, ctx, sem.at[STREAMS])
    ctx_write = pltpu.make_async_copy(ctx, ctx_out, sem.at[STREAMS])
    writes = [
        pltpu.make_async_copy(grad.at[:, lo:hi], grad_out.at[:, lo:hi], sem.at[u])
        for u, (lo, hi) in enumerate(halves)
    ]
    for copy in (*parts, ctx_read):
        copy.start()
    for u in range(STREAMS):
        parts[u].wait()
        for g in range(4):
            lo = (4 * u + g) * lanes
            hi = min(lo + lanes, width)
            if lo >= hi:
                continue
            block = re[u, g // 2, g % 2].reshape(PAD, lanes)[:HEAD, : hi - lo]
            grad[:, lo:hi] = block.astype(F32) * scale
        writes[u].start()
        if u == 0:
            ctx_read.wait()
            ctx_write.start()
    for copy in (*writes, ctx_write):
        copy.wait()


def body(nz, features, segment_ids, projections, cotangent):
    ns = lax.axis_size("seq")
    ny = ns // 2
    width = features.shape[2]
    feat = features.reshape(2, HALF, width)
    seg = segment_ids.reshape(ns, ROWS)
    vmem = lambda *shape: pltpu.VMEM(shape, BF16)
    dma = lambda *shape: pltpu.SemaphoreType.DMA(shape)
    rows = 8 // nz
    lanes = GROUP // STREAMS
    reach = 2 * REACH + 1
    far = pl.BlockSpec(memory_space=pltpu.HBM)
    ctx, re = pl.pallas_call(
        functools.partial(kernel, nz),
        out_shape=(
            jax.ShapeDtypeStruct((ROWS, width), BF16),
            jax.ShapeDtypeStruct((STREAMS, 2, 2, 8, 16, lanes), BF16),
        ),
        in_specs=[far] * 4,
        out_specs=[far, far],
        scratch_shapes=[
            pltpu.VMEM((ns, ROWS), jnp.int32),
            vmem(ny, 2, HALF, width),
            vmem(3, HEAD, width),
            vmem(2, 3, 2, 2, HALF // 2, width),
            vmem(ROWS, width),
            vmem(ny, 2, ROWS, PAD),
            vmem(ny, ROWS, PAD),
            vmem(ny, 2, ROWS, PAD),
            vmem(ns, 3, ROWS, PAD),
            vmem(ny, 3, ROWS, PAD),
            pltpu.VMEM((ns, ROWS, ROWS), F32),
            vmem(ny, reach, 2 * ROWS, 2 * ROWS),
            pltpu.VMEM((ny, 2 * ROWS, PAD), F32),
            pltpu.VMEM((ny, PAD, 2 * ROWS), F32),
            vmem(ny, 2, ROWS, PAD),
            vmem(ny, ROWS, PAD),
            vmem(ny, 2, ROWS, PAD),
            vmem(ROWS, width),
            vmem(2, ny, PAD, ROWS),
            vmem(ny, PAD, ROWS),
            vmem(STREAMS, 2, 2, 2, 8, 16, lanes),
            vmem(STREAMS, 2, 2, 8, 16, lanes),
            vmem(STREAMS, 2, 2, 8, 16, lanes),
            vmem(STREAMS, 3, 8, 16, lanes),
            vmem(STREAMS, 8, 16, lanes),
            vmem(STREAMS, nz, rows, 16, lanes),
            vmem(STREAMS, rows, 16, lanes),
            vmem(STREAMS, 2, 2, 8, 16, lanes),
            dma(13),
            dma(2, ny - 1),
            dma(1 + max(3, STREAMS)),
            dma(3), dma(3), dma(),
            dma(3),
            dma(), dma(ny - 2),
            dma(), dma(), dma(),
            dma(STREAMS, 2),
            dma(STREAMS), dma(STREAMS), dma(STREAMS),
            dma(STREAMS, 2),
        ],
        compiler_params=pltpu.CompilerParams(
            collective_id=0, has_side_effects=True, vmem_limit_bytes=62 * 1024 * 1024
        ),
    )(feat, projections, cotangent[0], seg)
    ctx, grad = pl.pallas_call(
        functools.partial(finish, 1.0 / (4 * nz)),
        out_shape=(
            jax.ShapeDtypeStruct((ROWS, width), BF16),
            jax.ShapeDtypeStruct((HEAD, width), F32),
        ),
        in_specs=[far, far],
        out_specs=[far, far],
        scratch_shapes=[
            vmem(ROWS, width),
            vmem(STREAMS, 2, 2, 8, 16, lanes),
            pltpu.VMEM((HEAD, width), F32),
            dma(STREAMS + 1),
        ],
    )(ctx, re)
    return (ctx[None], grad)


def solution(mesh):
    in_specs = (P("dp", "seq", None), P("dp", None), P(None, "seq", None), P("dp", "seq", None))
    out_specs = (P("dp", "seq", None), P("seq", None))
    step = functools.partial(body, mesh.shape["dp"] // 4)
    return jax.shard_map(step, mesh=mesh, in_specs=in_specs, out_specs=out_specs, check_vma=False)
```

```python
import functools

import jax
import jax.numpy as jnp
from jax import lax
from jax.experimental import pallas as pl
from jax.experimental.pallas import tpu as pltpu
from jax.sharding import PartitionSpec as P

HEAD = 120
PAD = 128
ROWS = 128
HALF = 64
REACH = 2
STREAMS = 2
GROUP = 512
RING, WALL, DX, QSENT, DSENT, XSENT, VSENT, CSENT, ASENT, BSENT, ZSENT, TSENT, ESENT = range(13)
LOG2E = 1.4426950408889634
MESH = pl.DeviceIdType.MESH
NT = (((1,), (1,)), ((), ()))
NN = (((1,), (0,)), ((), ()))
TN = (((0,), (0,)), ((), ()))
F32 = jnp.float32
BF16 = jnp.bfloat16


def kernel(
    nz, feat, w, cot, seg_in, ctx_out, re_out,
    seg, G, WR, WA, CO, CT, XO, DO, QKV, QS, SEGC, EB, INV, VRT, CP, XC, CR, CF,
    AB, AS, PB, RA, PA, RB, PC, RC, PD, RE,
    near, sent, ring_r, loc, w_r, wz_r, wc_r, qs_r, dx_r, do_r, xc_r, cx_r, vr_r, a_r, b_r, c_r, d_r, e_r,
):
    ny = G.shape[0]
    ns = 2 * ny
    width = feat.shape[2]
    dp, sq = lax.axis_index("dp"), lax.axis_index("seq")
    core = lax.rem(dp, 2)
    xhi = lax.rem(lax.div(dp, 2), 2)
    z = lax.div(dp, 4)
    zlo = lax.rem(z, 2)
    y = lax.div(sq, 2)
    xlo = lax.rem(sq, 2)
    other = 1 - core
    peer_x = sq + 1 - 2 * xlo
    peer_core = dp + 1 - 2 * core
    peer_xhi = dp + 2 - 4 * xhi
    peer_z = dp + 4 - 8 * zlo

    def remote(src, dst, kind, rsem, dev):
        return pltpu.make_async_remote_copy(
            src_ref=src,
            dst_ref=dst,
            send_sem=sent.at[kind],
            recv_sem=rsem,
            device_id=dev,
            device_id_type=MESH,
        )

    def landed(ref, sem):
        pltpu.make_async_copy(ref, ref, sem).wait()

    own_feat = pltpu.make_async_copy(feat, G.at[y], loc.at[0])
    own_w = pltpu.make_async_copy(w, WR, loc.at[1])
    own_cot = pltpu.make_async_copy(cot, CO, loc.at[2])
    own_seg = pltpu.make_async_copy(seg_in, seg, loc.at[3])
    for copy in (own_feat, own_w, own_cot, own_seg):
        copy.start()

    barrier = pltpu.get_barrier_semaphore()

    def z_dev(d):
        return lax.rem(z + d + nz, nz) * 4 + lax.rem(dp, 4)

    y_near = [(dp, lax.rem(sq + d, ns)) for d in (2, ns - 2)]
    x_near = [(dp, peer_x), (peer_xhi, peer_x)]
    z_near = [(z_dev(d), sq) for d in (1, -1)]

    def hello(sem, devs):
        for dev in devs:
            pl.semaphore_signal(sem, inc=1, device_id=dev, device_id_type=MESH)

    hello(barrier, y_near + x_near + z_near + [(peer_core, sq)])
    pl.semaphore_wait(barrier, 7)

    def pass_on(step):
        if step:
            pl.semaphore_wait(near.at[step - 1], 2)
            pl.semaphore_wait(near.at[step + 2], 2)
        if step == 1:
            pl.semaphore_wait(near.at[6], 2)
        if step < 3:
            hello(near.at[step], y_near)
            hello(near.at[step + 3], z_near)
        if step == 0:
            hello(near.at[6], x_near)

    last = ny - 1

    def ring(dirn, k, at):
        hops = k // 2
        if dirn == 0:
            shard, half, to = lax.rem(at + ny - hops, ny), k % 2, lax.rem(sq + 2, ns)
        else:
            shard, half, to = lax.rem(at + hops, ny), 1 - k % 2, lax.rem(sq + ns - 2, ns)
        ref = G.at[shard, half]
        src = feat.at[half] if k < 2 else ref
        return remote(src, ref, RING, ring_r.at[dirn, k], (dp, to))

    def ring_send(dirn, k):
        return ring(dirn, k, y)

    def ring_recv(dirn, k):
        return ring(dirn, k, lax.rem(y + ny - 1, ny) if dirn == 0 else lax.rem(y + 1, ny))

    for k in range(2):
        for dirn in range(2):
            ring_send(dirn, k).start()
    pass_on(0)

    own_w.wait()
    quarter = HALF // 2
    for p in range(3):
        for c in range(4):
            lo = c * quarter
            hi = min(lo + quarter, HEAD)
            WA[0, p, c // 2, c % 2, 0 : hi - lo] = WR[p, lo:hi]
            if hi - lo < quarter:
                WA[0, p, c // 2, c % 2, hi - lo :] = jnp.zeros((quarter - hi + lo, width), BF16)
    def w_x(p):
        return remote(
            WA.at[0, p, core, zlo], WA.at[1, p, core, zlo], WALL, w_r.at[p], (dp, peer_x)
        )

    def w_z(p, at):
        ref = WA.at[1, p, core, at]
        return remote(ref, ref, WALL, wz_r.at[p], (peer_z, sq))

    def w_c(p, at):
        ref = WA.at[1, p, core, at]
        return remote(ref, ref, WALL, wc_r, (peer_core, sq))

    for p in range(3):
        w_x(p).start()

    own_cot.wait()
    for r in range(ny):
        left = CO[:, 2 * r * HEAD : (2 * r + 1) * HEAD]
        right = CO[:, (2 * r + 1) * HEAD : (2 * r + 2) * HEAD]
        XO[r] = jnp.zeros((ROWS, PAD), BF16)
        XO[r, :, 0:HEAD] = jnp.where(xlo == 0, right, left)
        CT[r, xlo] = jnp.zeros((ROWS, PAD), BF16)
        CT[r, xlo, :, 0:HEAD] = jnp.where(xlo == 0, left, right)

    def dx_copy(col):
        return remote(XO, CT.at[:, col], DX, dx_r, (dp, peer_x))

    dx_copy(xlo).start()

    def label_col(b, carry):
        row = seg[pl.ds(b, 1), :].astype(F32)
        SEGC[b] = jnp.broadcast_to(row, (ROWS, ROWS)).T
        return carry

    own_seg.wait()
    lax.fori_loop(0, ns, label_col, 0)
    VRT[...] = jnp.zeros_like(VRT)

    def at_y(d):
        return lax.rem(y + d + ny, ny)

    def arrive(k):
        for dirn in range(2):
            ring_recv(dirn, k).wait_recv()
            if k + 2 <= last - 1:
                ring_send(dirn, k + 2).start()

    arrive(0)
    pass_on(1)
    for p in range(3):
        w_x(p).wait_recv()
        w_z(p, zlo).start()
        w_c(p, zlo).start()
    for p in range(3):
        w_z(p, 1 - zlo).wait_recv()
        w_c(p, 1 - zlo).start()
    arrive(1)
    pass_on(2)

    def qs_copy(d):
        shard = at_y(d)
        n = 0 if abs(d) < 3 else abs(d) - 2
        return remote(QS.at[shard], QKV.at[2 * shard + xlo], QSENT, qs_r.at[n], (dp, peer_x))

    def project(d, apart=False):
        shard = at_y(d)
        x = G[shard].reshape(ROWS, width)

        def heads(wall):
            wall = wall.reshape(-1, width)
            return lax.dot_general(x, wall, NT, preferred_element_type=F32).astype(BF16)

        if apart:
            near, far = heads(WA[0]), heads(WA[1])
        else:
            both = heads(WA[...])
            near, far = both[:, : 3 * PAD], both[:, 3 * PAD :]
        for p in range(3):
            QS[shard, p] = far[:, p * PAD : (p + 1) * PAD]
        qs_copy(d).start()
        for p in range(3):
            QKV[2 * shard + xlo, p] = near[:, p * PAD : (p + 1) * PAD]

    def do_copy(d):
        r = at_y(d)
        n = 0 if abs(d) == 1 else (ny - d) % ny - 1
        return remote(CT.at[r], DO.at[y], DSENT, do_r.at[n], (dp, 2 * r + xlo))

    scale = HEAD ** (-0.5) * LOG2E

    def rows_of(p, r):
        return QKV[pl.ds(2 * r, 2), p].reshape(2 * ROWS, PAD)

    def attend(i):
        q = rows_of(0, i)
        col = SEGC[pl.ds(2 * i, 2)].reshape(2 * ROWS, PAD)
        parts = []
        for o in range(-REACH, REACH + 1):
            r = lax.rem(i + o + ny, ny)
            s = lax.dot_general(q, rows_of(1, r), NT, preferred_element_type=F32)
            for c in range(2):
                row = seg[pl.ds(2 * r + c, 1), :].astype(F32)
                parts.append(jnp.where(col == row, s[:, c * PAD : (c + 1) * PAD], -1e30))
        top = functools.reduce(jnp.maximum, parts)
        top = jnp.max(top, axis=1, keepdims=True)
        total = jnp.zeros((2 * ROWS, PAD), F32)
        ctx = jnp.zeros((2 * ROWS, PAD), F32)
        for n in range(2 * REACH + 1):
            left, right = (jnp.exp2((part - top) * scale) for part in parts[2 * n : 2 * n + 2])
            total += left + right
            e = jnp.concatenate([left.astype(BF16), right.astype(BF16)], axis=1)
            EB[i, n] = e
            r = lax.rem(i + n - REACH + ny, ny)
            ctx += lax.dot_general(e, rows_of(2, r), NN, preferred_element_type=F32)
        inv = jnp.broadcast_to(1.0 / jnp.sum(total, axis=1, keepdims=True), (2 * ROWS, PAD))
        INV[i] = inv
        ctx = (ctx * inv).astype(BF16)
        left, right = ctx[:ROWS], ctx[ROWS:]
        XC[i] = jnp.where(xlo == 0, right, left)
        xc_copy(i, xlo).start()
        CP[i, xlo] = jnp.where(xlo == 0, left, right)

    def xc_copy(i, head):
        return remote(XC.at[i], CP.at[i, head], XSENT, xc_r, (dp, peer_x))

    def attend_at(d, carry):
        attend(at_y(d))
        return carry

    arrive(2)
    pass_on(3)
    own_feat.wait()
    landed(WA.at[1, :, other], wc_r)
    project(0)
    arrive(3)
    project(1)
    project(-1)
    arrive(4)
    dx_copy(1 - xlo).wait_recv()
    for d in (1, -1, -2, -3):
        do_copy(d).start()
    DO[y] = CT[y]
    project(2)
    project(-2)
    arrive(5)
    for d in (4, 3, 2):
        do_copy(d).start()
    project(3)
    project(-3)
    landed(QS.at[pl.ds(0, 5)], qs_r.at[0])
    attend(y)
    arrive(6)
    project(4, apart=True)
    landed(QS.at[pl.ds(0, 2)], qs_r.at[1])
    lax.fori_loop(0, 2, lambda t, carry: attend_at(1 + 6 * t, carry), 0)

    def vr_copy(r):
        return remote(AS.at[r], AB.at[1, r], VSENT, vr_r, (dp, peer_x))

    def value_rows_out(r):
        v = VRT[r].astype(BF16)
        left, right = v[:, :PAD], v[:, PAD:]
        AS[r] = jnp.where(xlo == 0, right, left)
        vr_copy(r).start()
        AB[0, r] = jnp.where(xlo == 0, left, right)

    def value_step(i):
        up = DO[i].reshape(2 * ROWS, PAD).astype(F32) * INV[i]
        up = up.astype(BF16)
        for n in range(2 * REACH + 1):
            r = lax.rem(i + n - REACH + ny, ny)
            VRT[r] += lax.dot_general(up, EB[i, n], TN, preferred_element_type=F32)

    def value_at(d, carry):
        value_step(at_y(d))
        return carry

    value_step(y)
    landed(DO.at[pl.ds(0, 2)], do_r.at[0])
    lax.fori_loop(0, 2, lambda t, carry: value_at(1 + 6 * t, carry), 0)
    landed(QS.at[0], qs_r.at[2])

    def far_rows(d, carry):
        attend(at_y(d))

        @pl.when(d > 2)
        def _():
            landed(DO.at[at_y(d - 1)], do_r.at[d - 2])
            value_step(at_y(d - 1))

        @pl.when(d > 3)
        def _():
            value_rows_out(at_y(d - 3))

        return carry

    lax.fori_loop(2, ny - 1, far_rows, 0)
    landed(DO.at[at_y(-2)], do_r.at[ny - 3])
    value_step(at_y(-2))
    for d in (4, 5, 6, 7, 0):
        value_rows_out(at_y(d))

    def cx_copy(r):
        return remote(CP.at[r], CR.at[y], CSENT, cx_r, (dp, 2 * r + xlo))

    lanes = GROUP // STREAMS

    def a_copy(u, h):
        return remote(PB.at[u, other, h], RA.at[u, h], ASENT, a_r.at[u, h], (peer_core, sq))

    def product(h):
        lhs = jnp.concatenate([AB[h, t] for t in range(ny)], axis=1)
        for u in range(STREAMS):
            lo = 4 * u * lanes
            hi = min(lo + 4 * lanes, width)
            rhs = G[:, :, :, lo:hi].reshape(ny * ROWS, hi - lo)
            part = lax.dot_general(lhs, rhs, NN, preferred_element_type=F32).astype(BF16)
            if hi - lo < 4 * lanes:
                part = jnp.concatenate([part, jnp.zeros((PAD, 4 * lanes - hi + lo), BF16)], axis=1)
            for g in range(4):
                block = part[:, g * lanes : (g + 1) * lanes]
                PB[u, g % 2, h, g // 2] = block.reshape(8, 16, lanes)
            a_copy(u, h).start()

    def b_copy(u, n):
        h, g = (1, xhi) if n == 0 else (0, 1 - xhi) if n == 1 else (1, 1 - xhi)
        dev = (dp if n == 0 else peer_xhi, sq if n == 1 else peer_x)
        return remote(PA.at[u, h, g], RB.at[u, n], BSENT, b_r.at[u], dev)

    def core_sum(u, h):
        a_copy(u, h).wait_recv()
        for g in range(2):
            PA[u, h, g] = (PB[u, core, h, g].astype(F32) + RA[u, h, g].astype(F32)).astype(BF16)

    product(0)
    for u in range(STREAMS):
        core_sum(u, 0)
        b_copy(u, 1).start()
    landed(AS, vr_r)
    product(1)
    landed(XC, xc_r)
    for d in (4, 3, -3, 2, -2, 1, -1):
        cx_copy(at_y(d)).start()
    CR[y] = CP[y]
    for u in range(STREAMS):
        core_sum(u, 1)
        b_copy(u, 2).start()
        b_copy(u, 0).start()

    rows = 8 // nz

    def c_copy(u, d):
        to = lax.rem(z + d, nz)
        return remote(
            PC.at[u, pl.ds(to * rows, rows)], RC.at[u, d], ZSENT, c_r.at[u], (z_dev(d), sq)
        )

    by_reach = sorted(range(1, nz), key=lambda d: -min(d, nz - d))
    for u in range(STREAMS):
        total = PA[u, 0, xhi].astype(F32)
        landed(RB.at[u], b_r.at[u])
        for n in range(3):
            total += RB[u, n].astype(F32)
        PC[u] = total.astype(BF16)
        for d in by_reach:
            c_copy(u, d).start()

    def d_copy(u, d):
        into = RE.at[u, xhi, core, pl.ds(z * rows, rows)]
        return remote(PD.at[u], into, TSENT, d_r.at[u], (z_dev(d), sq))

    for u in range(STREAMS):
        total = PC[u, pl.ds(z * rows, rows)].astype(F32)
        landed(RC.at[u, pl.ds(1, nz - 1)], c_r.at[u])
        for d in range(1, nz):
            total += RC[u, d].astype(F32)
        PD[u] = total.astype(BF16)
        for d in by_reach:
            d_copy(u, d).start()
        RE[u, xhi, core, pl.ds(z * rows, rows)] = total.astype(BF16)

    def e_copy(u, n, recv=False):
        c = other if recv and n > 0 else core
        hi = 1 - xhi if (n == 2) != (recv and n == 0) else xhi
        ref = RE.at[u, hi, c]
        dev = (peer_xhi if n == 0 else peer_core, sq)
        return remote(ref, ref, ESENT, e_r.at[u, min(n, 1)], dev)

    landed(CR.at[pl.ds(0, ny - 1)], cx_r)
    for h in range(ns):
        CF[:, h * HEAD : (h + 1) * HEAD] = CR[h // 2, h % 2, :, 0:HEAD]
    ctx_copy = pltpu.make_async_copy(CF, ctx_out, loc.at[0])
    ctx_copy.start()

    for u in range(STREAMS):
        landed(RC.at[u, pl.ds(1, nz - 1)], d_r.at[u])
        e_copy(u, 0).start()
        e_copy(u, 1).start()
    for u in range(STREAMS):
        e_copy(u, 0, True).wait_recv()
        e_copy(u, 2).start()
    re_copies = [pltpu.make_async_copy(RE.at[u], re_out.at[u], loc.at[1 + u]) for u in range(STREAMS)]
    for u in range(STREAMS):
        landed(RE.at[u, :, other], e_r.at[u, 1])
        re_copies[u].start()

    for kind, ref in (
        (RING, G.at[pl.ds(0, last)]),
        (WALL, WA.at[1]),
        (DX, XO),
        (QSENT, QS),
        (DSENT, CT.at[pl.ds(0, ny - 1)]),
        (XSENT, XC),
        (VSENT, AS),
        (CSENT, CP.at[pl.ds(0, ny - 1)]),
        (ASENT, RA),
        (BSENT, RB),
        (ZSENT, RC.at[:, pl.ds(1, nz - 1)]),
        (TSENT, RC.at[:, pl.ds(1, nz - 1)]),
        (ESENT, RB),
    ):
        landed(ref, sent.at[kind])
    ctx_copy.wait()
    for copy in re_copies:
        copy.wait()


def finish(scale, ctx_in, re_in, ctx_out, grad_out, ctx, re, grad, sem):
    lanes = GROUP // STREAMS
    width = grad_out.shape[1]
    halves = [(4 * lanes * u, min(4 * lanes * (u + 1), width)) for u in range(STREAMS)]
    parts = [pltpu.make_async_copy(re_in.at[u], re.at[u], sem.at[u]) for u in range(STREAMS)]
    ctx_read = pltpu.make_async_copy(ctx_in, ctx, sem.at[STREAMS])
    ctx_write = pltpu.make_async_copy(ctx, ctx_out, sem.at[STREAMS])
    writes = [
        pltpu.make_async_copy(grad.at[:, lo:hi], grad_out.at[:, lo:hi], sem.at[u])
        for u, (lo, hi) in enumerate(halves)
    ]
    for copy in (*parts, ctx_read):
        copy.start()
    for u in range(STREAMS):
        parts[u].wait()
        for g in range(4):
            lo = (4 * u + g) * lanes
            hi = min(lo + lanes, width)
            if lo >= hi:
                continue
            block = re[u, g // 2, g % 2].reshape(PAD, lanes)[:HEAD, : hi - lo]
            grad[:, lo:hi] = block.astype(F32) * scale
        writes[u].start()
        if u == 0:
            ctx_read.wait()
            ctx_write.start()
    for copy in (*writes, ctx_write):
        copy.wait()


def body(nz, features, segment_ids, projections, cotangent):
    ns = lax.axis_size("seq")
    ny = ns // 2
    width = features.shape[2]
    feat = features.reshape(2, HALF, width)
    seg = segment_ids.reshape(ns, ROWS)
    vmem = lambda *shape: pltpu.VMEM(shape, BF16)
    dma = lambda *shape: pltpu.SemaphoreType.DMA(shape)
    rows = 8 // nz
    lanes = GROUP // STREAMS
    reach = 2 * REACH + 1
    far = pl.BlockSpec(memory_space=pltpu.HBM)
    ctx, re = pl.pallas_call(
        functools.partial(kernel, nz),
        out_shape=(
            jax.ShapeDtypeStruct((ROWS, width), BF16),
            jax.ShapeDtypeStruct((STREAMS, 2, 2, 8, 16, lanes), BF16),
        ),
        in_specs=[far] * 4,
        out_specs=[far, far],
        scratch_shapes=[
            pltpu.VMEM((ns, ROWS), jnp.int32),
            vmem(ny, 2, HALF, width),
            vmem(3, HEAD, width),
            vmem(2, 3, 2, 2, HALF // 2, width),
            vmem(ROWS, width),
            vmem(ny, 2, ROWS, PAD),
            vmem(ny, ROWS, PAD),
            vmem(ny, 2, ROWS, PAD),
            vmem(ns, 3, ROWS, PAD),
            vmem(ny, 3, ROWS, PAD),
            pltpu.VMEM((ns, ROWS, ROWS), F32),
            vmem(ny, reach, 2 * ROWS, 2 * ROWS),
            pltpu.VMEM((ny, 2 * ROWS, PAD), F32),
            pltpu.VMEM((ny, PAD, 2 * ROWS), F32),
            vmem(ny, 2, ROWS, PAD),
            vmem(ny, ROWS, PAD),
            vmem(ny, 2, ROWS, PAD),
            vmem(ROWS, width),
            vmem(2, ny, PAD, ROWS),
            vmem(ny, PAD, ROWS),
            vmem(STREAMS, 2, 2, 2, 8, 16, lanes),
            vmem(STREAMS, 2, 2, 8, 16, lanes),
            vmem(STREAMS, 2, 2, 8, 16, lanes),
            vmem(STREAMS, 3, 8, 16, lanes),
            vmem(STREAMS, 8, 16, lanes),
            vmem(STREAMS, nz, rows, 16, lanes),
            vmem(STREAMS, rows, 16, lanes),
            vmem(STREAMS, 2, 2, 8, 16, lanes),
            pltpu.SemaphoreType.REGULAR((7,)),
            dma(13),
            dma(2, ny - 1),
            dma(1 + max(3, STREAMS)),
            dma(3), dma(3), dma(),
            dma(3),
            dma(), dma(ny - 2),
            dma(), dma(), dma(),
            dma(STREAMS, 2),
            dma(STREAMS), dma(STREAMS), dma(STREAMS),
            dma(STREAMS, 2),
        ],
        compiler_params=pltpu.CompilerParams(
            collective_id=0, has_side_effects=True, vmem_limit_bytes=62 * 1024 * 1024
        ),
    )(feat, projections, cotangent[0], seg)
    ctx, grad = pl.pallas_call(
        functools.partial(finish, 1.0 / (4 * nz)),
        out_shape=(
            jax.ShapeDtypeStruct((ROWS, width), BF16),
            jax.ShapeDtypeStruct((HEAD, width), F32),
        ),
        in_specs=[far, far],
        out_specs=[far, far],
        scratch_shapes=[
            vmem(ROWS, width),
            vmem(STREAMS, 2, 2, 8, 16, lanes),
            pltpu.VMEM((HEAD, width), F32),
            dma(STREAMS + 1),
        ],
    )(ctx, re)
    return (ctx[None], grad)


def solution(mesh):
    in_specs = (P("dp", "seq", None), P("dp", None), P(None, "seq", None), P("dp", "seq", None))
    out_specs = (P("dp", "seq", None), P("seq", None))
    step = functools.partial(body, mesh.shape["dp"] // 4)
    return jax.shard_map(step, mesh=mesh, in_specs=in_specs, out_specs=out_specs, check_vma=False)
```

```python
import functools

import jax
import jax.numpy as jnp
from jax import lax
from jax.experimental import pallas as pl
from jax.experimental.pallas import tpu as pltpu
from jax.sharding import PartitionSpec as P

HEAD = 120
PAD = 128
ROWS = 128
HALF = 64
REACH = 2
STREAMS = 4
GROUP = 512
RING, WALL, DX, QSENT, DSENT, XSENT, VSENT, CSENT, ASENT, BSENT, ZSENT, TSENT, ESENT = range(13)
LOG2E = 1.4426950408889634
MESH = pl.DeviceIdType.MESH
NT = (((1,), (1,)), ((), ()))
NN = (((1,), (0,)), ((), ()))
TN = (((0,), (0,)), ((), ()))
F32 = jnp.float32
BF16 = jnp.bfloat16


def kernel(
    nz, feat, w, cot, seg_in, ctx_out, re_out,
    seg, G, WR, WA, CO, CT, XO, DO, QKV, QS, SEGC, EB, INV, VRT, CP, XC, CR, CF,
    AB, AS, PB, RA, PA, RB, PC, RC, PD, RE,
    near, sent, ring_r, loc, w_r, wz_r, wc_r, qs_r, dx_r, do_r, xc_r, cx_r, vr_r, a_r, b_r, c_r, d_r, e_r,
):
    ny = G.shape[0]
    ns = 2 * ny
    width = feat.shape[2]
    dp, sq = lax.axis_index("dp"), lax.axis_index("seq")
    core = lax.rem(dp, 2)
    xhi = lax.rem(lax.div(dp, 2), 2)
    z = lax.div(dp, 4)
    zlo = lax.rem(z, 2)
    y = lax.div(sq, 2)
    xlo = lax.rem(sq, 2)
    other = 1 - core
    peer_x = sq + 1 - 2 * xlo
    peer_core = dp + 1 - 2 * core
    peer_xhi = dp + 2 - 4 * xhi
    peer_z = dp + 4 - 8 * zlo

    def remote(src, dst, kind, rsem, dev):
        return pltpu.make_async_remote_copy(
            src_ref=src,
            dst_ref=dst,
            send_sem=sent.at[kind],
            recv_sem=rsem,
            device_id=dev,
            device_id_type=MESH,
        )

    def landed(ref, sem):
        pltpu.make_async_copy(ref, ref, sem).wait()

    own_feat = pltpu.make_async_copy(feat, G.at[y], loc.at[0])
    own_w = pltpu.make_async_copy(w, WR, loc.at[1])
    own_cot = pltpu.make_async_copy(cot, CO, loc.at[2])
    own_seg = pltpu.make_async_copy(seg_in, seg, loc.at[3])
    for copy in (own_feat, own_w, own_cot, own_seg):
        copy.start()

    barrier = pltpu.get_barrier_semaphore()

    def z_dev(d):
        return lax.rem(z + d + nz, nz) * 4 + lax.rem(dp, 4)

    y_near = [(dp, lax.rem(sq + d, ns)) for d in (2, ns - 2)]
    x_near = [(dp, peer_x), (peer_xhi, peer_x)]
    z_near = [(z_dev(d), sq) for d in (1, -1)]

    def hello(sem, devs):
        for dev in devs:
            pl.semaphore_signal(sem, inc=1, device_id=dev, device_id_type=MESH)

    hello(barrier, y_near + x_near + z_near + [(peer_core, sq)])
    pl.semaphore_wait(barrier, 7)

    def pass_on(step):
        if step:
            pl.semaphore_wait(near.at[step - 1], 2)
            pl.semaphore_wait(near.at[step + 2], 2)
        if step == 1:
            pl.semaphore_wait(near.at[6], 2)
        if step < 3:
            hello(near.at[step], y_near)
            hello(near.at[step + 3], z_near)
        if step == 0:
            hello(near.at[6], x_near)

    last = ny - 1

    def ring(dirn, k, at):
        hops = k // 2
        if dirn == 0:
            shard, half, to = lax.rem(at + ny - hops, ny), k % 2, lax.rem(sq + 2, ns)
        else:
            shard, half, to = lax.rem(at + hops, ny), 1 - k % 2, lax.rem(sq + ns - 2, ns)
        ref = G.at[shard, half]
        src = feat.at[half] if k < 2 else ref
        return remote(src, ref, RING, ring_r.at[dirn, k], (dp, to))

    def ring_send(dirn, k):
        return ring(dirn, k, y)

    def ring_recv(dirn, k):
        return ring(dirn, k, lax.rem(y + ny - 1, ny) if dirn == 0 else lax.rem(y + 1, ny))

    for k in range(2):
        for dirn in range(2):
            ring_send(dirn, k).start()
    pass_on(0)

    own_w.wait()
    quarter = HALF // 2
    for p in range(3):
        for c in range(4):
            lo = c * quarter
            hi = min(lo + quarter, HEAD)
            WA[0, p, c // 2, c % 2, 0 : hi - lo] = WR[p, lo:hi]
            if hi - lo < quarter:
                WA[0, p, c // 2, c % 2, hi - lo :] = jnp.zeros((quarter - hi + lo, width), BF16)
    def w_x(p):
        return remote(
            WA.at[0, p, core, zlo], WA.at[1, p, core, zlo], WALL, w_r.at[p], (dp, peer_x)
        )

    def w_z(p, at):
        ref = WA.at[1, p, core, at]
        return remote(ref, ref, WALL, wz_r.at[p], (peer_z, sq))

    def w_c(p, at):
        ref = WA.at[1, p, core, at]
        return remote(ref, ref, WALL, wc_r, (peer_core, sq))

    for p in range(3):
        w_x(p).start()

    own_cot.wait()
    for r in range(ny):
        left = CO[:, 2 * r * HEAD : (2 * r + 1) * HEAD]
        right = CO[:, (2 * r + 1) * HEAD : (2 * r + 2) * HEAD]
        XO[r] = jnp.zeros((ROWS, PAD), BF16)
        XO[r, :, 0:HEAD] = jnp.where(xlo == 0, right, left)
        CT[r, xlo] = jnp.zeros((ROWS, PAD), BF16)
        CT[r, xlo, :, 0:HEAD] = jnp.where(xlo == 0, left, right)

    def dx_copy(col):
        return remote(XO, CT.at[:, col], DX, dx_r, (dp, peer_x))

    dx_copy(xlo).start()

    def label_col(b, carry):
        row = seg[pl.ds(b, 1), :].astype(F32)
        SEGC[b] = jnp.broadcast_to(row, (ROWS, ROWS)).T
        return carry

    own_seg.wait()
    lax.fori_loop(0, ns, label_col, 0)
    VRT[...] = jnp.zeros_like(VRT)

    def at_y(d):
        return lax.rem(y + d + ny, ny)

    def arrive(k):
        for dirn in range(2):
            ring_recv(dirn, k).wait_recv()
            if k + 2 <= last - 1:
                ring_send(dirn, k + 2).start()

    arrive(0)
    pass_on(1)
    for p in range(3):
        w_x(p).wait_recv()
        w_z(p, zlo).start()
        w_c(p, zlo).start()
    arrive(1)
    pass_on(2)
    for p in range(3):
        w_z(p, 1 - zlo).wait_recv()
        w_c(p, 1 - zlo).start()

    def qs_copy(d):
        shard = at_y(d)
        n = 0 if abs(d) < 3 else abs(d) - 2
        return remote(QS.at[shard], QKV.at[2 * shard + xlo], QSENT, qs_r.at[n], (dp, peer_x))

    def project(d, apart=False):
        shard = at_y(d)
        x = G[shard].reshape(ROWS, width)

        def heads(wall):
            wall = wall.reshape(-1, width)
            return lax.dot_general(x, wall, NT, preferred_element_type=F32).astype(BF16)

        lane = lax.broadcasted_iota(jnp.int32, (ROWS, PAD), 1)
        one = jnp.where(lane == HEAD, 1.0, 0.0).astype(BF16)

        def block(cols, p):
            part = cols[:, p * PAD : (p + 1) * PAD]
            return part + one if p == 2 else part

        both = None if apart else heads(WA[...])
        far = heads(WA[1]) if apart else both[:, 3 * PAD :]
        for p in range(3):
            QS[shard, p] = block(far, p)
        qs_copy(d).start()
        near = heads(WA[0]) if apart else both[:, : 3 * PAD]
        for p in range(3):
            QKV[2 * shard + xlo, p] = block(near, p)

    def do_copy(d):
        r = at_y(d)
        n = 0 if abs(d) == 1 else (ny - d) % ny - 1
        return remote(CT.at[r], DO.at[y], DSENT, do_r.at[n], (dp, 2 * r + xlo))

    scale = HEAD ** (-0.5) * LOG2E

    def rows_of(p, r):
        return QKV[pl.ds(2 * r, 2), p].reshape(2 * ROWS, PAD)

    def attend(i):
        q = rows_of(0, i)
        col = SEGC[pl.ds(2 * i, 2)].reshape(2 * ROWS, PAD)
        parts = []
        for o in range(-REACH, REACH + 1):
            r = lax.rem(i + o + ny, ny)
            s = lax.dot_general(q, rows_of(1, r), NT, preferred_element_type=F32)
            for c in range(2):
                row = seg[pl.ds(2 * r + c, 1), :].astype(F32)
                parts.append(jnp.where(col == row, s[:, c * PAD : (c + 1) * PAD], -1e30))
        top = functools.reduce(jnp.maximum, parts)
        top = jnp.max(top, axis=1, keepdims=True)
        ctx = jnp.zeros((2 * ROWS, PAD), F32)
        for n in range(2 * REACH + 1):
            left, right = (jnp.exp2((part - top) * scale) for part in parts[2 * n : 2 * n + 2])
            e = jnp.concatenate([left.astype(BF16), right.astype(BF16)], axis=1)
            EB[i, n] = e
            r = lax.rem(i + n - REACH + ny, ny)
            ctx += lax.dot_general(e, rows_of(2, r), NN, preferred_element_type=F32)
        inv = jnp.broadcast_to(1.0 / ctx[:, HEAD : HEAD + 1], (2 * ROWS, PAD))
        INV[i] = inv
        ctx = (ctx * inv).astype(BF16)
        left, right = ctx[:ROWS], ctx[ROWS:]
        XC[i] = jnp.where(xlo == 0, right, left)
        xc_copy(i, xlo).start()
        CP[i, xlo] = jnp.where(xlo == 0, left, right)

    def xc_copy(i, head):
        return remote(XC.at[i], CP.at[i, head], XSENT, xc_r, (dp, peer_x))

    def attend_at(d, carry):
        attend(at_y(d))
        return carry

    arrive(2)
    pass_on(3)
    own_feat.wait()
    landed(WA.at[1, :, other], wc_r)
    project(0)
    arrive(3)
    project(1)
    project(-1)
    arrive(4)
    dx_copy(1 - xlo).wait_recv()
    for d in (1, -1, -2, -3):
        do_copy(d).start()
    DO[y] = CT[y]
    project(2)
    project(-2)
    arrive(5)
    for d in (4, 3, 2):
        do_copy(d).start()
    project(3)
    project(-3)
    landed(QS.at[pl.ds(0, 5)], qs_r.at[0])
    attend(y)
    arrive(6)
    project(4, apart=True)
    landed(QS.at[pl.ds(0, 2)], qs_r.at[1])
    lax.fori_loop(0, 2, lambda t, carry: attend_at(1 + 6 * t, carry), 0)

    def vr_copy(r):
        return remote(AS.at[r], AB.at[1, r], VSENT, vr_r, (dp, peer_x))

    def value_rows_out(r):
        v = VRT[r].astype(BF16)
        left, right = v[:, :PAD], v[:, PAD:]
        AS[r] = jnp.where(xlo == 0, right, left)
        vr_copy(r).start()
        AB[0, r] = jnp.where(xlo == 0, left, right)

    def value_step(i):
        up = DO[i].reshape(2 * ROWS, PAD).astype(F32) * INV[i]
        up = up.astype(BF16)
        for n in range(2 * REACH + 1):
            r = lax.rem(i + n - REACH + ny, ny)
            VRT[r] += lax.dot_general(up, EB[i, n], TN, preferred_element_type=F32)

    def value_at(d, carry):
        value_step(at_y(d))
        return carry

    value_step(y)
    landed(DO.at[pl.ds(0, 2)], do_r.at[0])
    lax.fori_loop(0, 2, lambda t, carry: value_at(1 + 6 * t, carry), 0)
    landed(QS.at[0], qs_r.at[2])

    def far_rows(d, carry):
        attend(at_y(d))

        @pl.when(d > 2)
        def _():
            landed(DO.at[at_y(d - 1)], do_r.at[d - 2])
            value_step(at_y(d - 1))

        @pl.when(d > 3)
        def _():
            value_rows_out(at_y(d - 3))

        return carry

    lax.fori_loop(2, ny - 1, far_rows, 0)
    landed(DO.at[at_y(-2)], do_r.at[ny - 3])
    value_step(at_y(-2))
    for d in (4, 5, 6, 7, 0):
        value_rows_out(at_y(d))

    def cx_copy(r):
        return remote(CP.at[r], CR.at[y], CSENT, cx_r, (dp, 2 * r + xlo))

    lanes = GROUP // STREAMS

    def a_copy(u, h):
        return remote(PB.at[u, other, h], RA.at[u, h], ASENT, a_r.at[u, h], (peer_core, sq))

    def product(h):
        lhs = jnp.concatenate([AB[h, t] for t in range(ny)], axis=1)
        for u in range(STREAMS):
            lo = 4 * u * lanes
            hi = min(lo + 4 * lanes, width)
            rhs = G[:, :, :, lo:hi].reshape(ny * ROWS, hi - lo)
            part = lax.dot_general(lhs, rhs, NN, preferred_element_type=F32).astype(BF16)
            if hi - lo < 4 * lanes:
                part = jnp.concatenate([part, jnp.zeros((PAD, 4 * lanes - hi + lo), BF16)], axis=1)
            for g in range(4):
                block = part[:, g * lanes : (g + 1) * lanes]
                PB[u, g % 2, h, g // 2] = block.reshape(8, 16, lanes)
            a_copy(u, h).start()

    def b_copy(u, n):
        h, g = (1, xhi) if n == 0 else (0, 1 - xhi) if n == 1 else (1, 1 - xhi)
        dev = (dp if n == 0 else peer_xhi, sq if n == 1 else peer_x)
        return remote(PA.at[u, h, g], RB.at[u, n], BSENT, b_r.at[u], dev)

    def core_sum(u, h):
        a_copy(u, h).wait_recv()
        for g in range(2):
            PA[u, h, g] = (PB[u, core, h, g].astype(F32) + RA[u, h, g].astype(F32)).astype(BF16)

    product(0)
    for u in range(STREAMS):
        core_sum(u, 0)
        b_copy(u, 1).start()
    landed(AS, vr_r)
    product(1)
    landed(XC, xc_r)
    for d in (4, 3, -3, 2, -2, 1, -1):
        cx_copy(at_y(d)).start()
    CR[y] = CP[y]
    for u in range(STREAMS):
        core_sum(u, 1)
        b_copy(u, 2).start()
        b_copy(u, 0).start()

    rows = 8 // nz

    def c_copy(u, d):
        to = lax.rem(z + d, nz)
        return remote(
            PC.at[u, pl.ds(to * rows, rows)], RC.at[u, d], ZSENT, c_r.at[u], (z_dev(d), sq)
        )

    by_reach = sorted(range(1, nz), key=lambda d: -min(d, nz - d))
    for u in range(STREAMS):
        total = PA[u, 0, xhi].astype(F32)
        landed(RB.at[u], b_r.at[u])
        for n in range(3):
            total += RB[u, n].astype(F32)
        PC[u] = total.astype(BF16)
        for d in by_reach:
            c_copy(u, d).start()

    def reach_of(d):
        return 0 if min(d, nz - d) < 3 else 1

    def d_copy(u, d):
        into = RE.at[u, xhi, core, pl.ds(z * rows, rows)]
        return remote(PD.at[u], into, TSENT, d_r.at[u, reach_of(d)], (z_dev(d), sq))

    for u in range(STREAMS):
        total = PC[u, pl.ds(z * rows, rows)].astype(F32)
        landed(RC.at[u, pl.ds(1, nz - 1)], c_r.at[u])
        for d in range(1, nz):
            total += RC[u, d].astype(F32)
        PD[u] = total.astype(BF16)
        for d in by_reach:
            d_copy(u, d).start()
        RE[u, xhi, core, pl.ds(z * rows, rows)] = total.astype(BF16)

    def e_copy(u, n):
        ref = RE.at[u, xhi if n == 1 else 1 - xhi, core]
        return remote(ref, ref, ESENT, e_r.at[u, 1], (peer_core, sq))

    def e_piece(u, d):
        ref = RE.at[u, xhi, core, pl.ds(lax.rem(z + d, nz) * rows, rows)]
        return remote(ref, ref, ESENT, e_r.at[u, 0], (peer_xhi, sq))

    landed(CR.at[pl.ds(0, ny - 1)], cx_r)
    for h in range(ns):
        CF[:, h * HEAD : (h + 1) * HEAD] = CR[h // 2, h % 2, :, 0:HEAD]
    ctx_copy = pltpu.make_async_copy(CF, ctx_out, loc.at[0])
    ctx_copy.start()

    for part in range(2):
        steps = [d for d in range(1, nz) if reach_of(d) == part]
        for u in range(STREAMS):
            if part == 0:
                e_piece(u, 0).start()
            landed(RC.at[u, pl.ds(1, len(steps))], d_r.at[u, part])
            for d in steps:
                e_piece(u, d).start()
            if part == 1:
                e_copy(u, 1).start()
    for u in range(STREAMS):
        landed(RE.at[u, 1 - xhi, core], e_r.at[u, 0])
        e_copy(u, 2).start()
    re_copies = [pltpu.make_async_copy(RE.at[u], re_out.at[u], loc.at[1 + u]) for u in range(STREAMS)]
    for u in range(STREAMS):
        landed(RE.at[u, :, other], e_r.at[u, 1])
        re_copies[u].start()

    for kind, ref in (
        (RING, G.at[pl.ds(0, last)]),
        (WALL, WA.at[1]),
        (DX, XO),
        (QSENT, QS),
        (DSENT, CT.at[pl.ds(0, ny - 1)]),
        (XSENT, XC),
        (VSENT, AS),
        (CSENT, CP.at[pl.ds(0, ny - 1)]),
        (ASENT, RA),
        (BSENT, RB),
        (ZSENT, RC.at[:, pl.ds(1, nz - 1)]),
        (TSENT, RC.at[:, pl.ds(1, nz - 1)]),
        (ESENT, RB),
    ):
        landed(ref, sent.at[kind])
    ctx_copy.wait()
    for copy in re_copies:
        copy.wait()


def finish(scale, ctx_in, re_in, ctx_out, grad_out, ctx, re, grad, sem):
    lanes = GROUP // STREAMS
    width = grad_out.shape[1]
    halves = [(4 * lanes * u, min(4 * lanes * (u + 1), width)) for u in range(STREAMS)]
    parts = [pltpu.make_async_copy(re_in.at[u], re.at[u], sem.at[u]) for u in range(STREAMS)]
    ctx_read = pltpu.make_async_copy(ctx_in, ctx, sem.at[STREAMS])
    ctx_write = pltpu.make_async_copy(ctx, ctx_out, sem.at[STREAMS])
    writes = [
        pltpu.make_async_copy(grad.at[:, lo:hi], grad_out.at[:, lo:hi], sem.at[u])
        for u, (lo, hi) in enumerate(halves)
    ]
    for copy in (*parts, ctx_read):
        copy.start()
    for u in range(STREAMS):
        parts[u].wait()
        for g in range(4):
            lo = (4 * u + g) * lanes
            hi = min(lo + lanes, width)
            if lo >= hi:
                continue
            block = re[u, g // 2, g % 2].reshape(PAD, lanes)[:HEAD, : hi - lo]
            grad[:, lo:hi] = block.astype(F32) * scale
        writes[u].start()
        if u == 0:
            ctx_read.wait()
            ctx_write.start()
    for copy in (*writes, ctx_write):
        copy.wait()


def body(nz, features, segment_ids, projections, cotangent):
    ns = lax.axis_size("seq")
    ny = ns // 2
    width = features.shape[2]
    feat = features.reshape(2, HALF, width)
    seg = segment_ids.reshape(ns, ROWS)
    vmem = lambda *shape: pltpu.VMEM(shape, BF16)
    dma = lambda *shape: pltpu.SemaphoreType.DMA(shape)
    rows = 8 // nz
    lanes = GROUP // STREAMS
    reach = 2 * REACH + 1
    far = pl.BlockSpec(memory_space=pltpu.HBM)
    ctx, re = pl.pallas_call(
        functools.partial(kernel, nz),
        out_shape=(
            jax.ShapeDtypeStruct((ROWS, width), BF16),
            jax.ShapeDtypeStruct((STREAMS, 2, 2, 8, 16, lanes), BF16),
        ),
        in_specs=[far] * 4,
        out_specs=[far, far],
        scratch_shapes=[
            pltpu.VMEM((ns, ROWS), jnp.int32),
            vmem(ny, 2, HALF, width),
            vmem(3, HEAD, width),
            vmem(2, 3, 2, 2, HALF // 2, width),
            vmem(ROWS, width),
            vmem(ny, 2, ROWS, PAD),
            vmem(ny, ROWS, PAD),
            vmem(ny, 2, ROWS, PAD),
            vmem(ns, 3, ROWS, PAD),
            vmem(ny, 3, ROWS, PAD),
            pltpu.VMEM((ns, ROWS, ROWS), F32),
            vmem(ny, reach, 2 * ROWS, 2 * ROWS),
            pltpu.VMEM((ny, 2 * ROWS, PAD), F32),
            pltpu.VMEM((ny, PAD, 2 * ROWS), F32),
            vmem(ny, 2, ROWS, PAD),
            vmem(ny, ROWS, PAD),
            vmem(ny, 2, ROWS, PAD),
            vmem(ROWS, width),
            vmem(2, ny, PAD, ROWS),
            vmem(ny, PAD, ROWS),
            vmem(STREAMS, 2, 2, 2, 8, 16, lanes),
            vmem(STREAMS, 2, 2, 8, 16, lanes),
            vmem(STREAMS, 2, 2, 8, 16, lanes),
            vmem(STREAMS, 3, 8, 16, lanes),
            vmem(STREAMS, 8, 16, lanes),
            vmem(STREAMS, nz, rows, 16, lanes),
            vmem(STREAMS, rows, 16, lanes),
            vmem(STREAMS, 2, 2, 8, 16, lanes),
            pltpu.SemaphoreType.REGULAR((7,)),
            dma(13),
            dma(2, ny - 1),
            dma(1 + max(3, STREAMS)),
            dma(3), dma(3), dma(),
            dma(3),
            dma(), dma(ny - 2),
            dma(), dma(), dma(),
            dma(STREAMS, 2),
            dma(STREAMS), dma(STREAMS), dma(STREAMS, 2),
            dma(STREAMS, 2),
        ],
        compiler_params=pltpu.CompilerParams(
            collective_id=0, has_side_effects=True, vmem_limit_bytes=62 * 1024 * 1024
        ),
    )(feat, projections, cotangent[0], seg)
    ctx, grad = pl.pallas_call(
        functools.partial(finish, 1.0 / (4 * nz)),
        out_shape=(
            jax.ShapeDtypeStruct((ROWS, width), BF16),
            jax.ShapeDtypeStruct((HEAD, width), F32),
        ),
        in_specs=[far, far],
        out_specs=[far, far],
        scratch_shapes=[
            vmem(ROWS, width),
            vmem(STREAMS, 2, 2, 8, 16, lanes),
            pltpu.VMEM((HEAD, width), F32),
            dma(STREAMS + 1),
        ],
    )(ctx, re)
    return (ctx[None], grad)


def solution(mesh):
    in_specs = (P("dp", "seq", None), P("dp", None), P(None, "seq", None), P("dp", "seq", None))
    out_specs = (P("dp", "seq", None), P("seq", None))
    step = functools.partial(body, mesh.shape["dp"] // 4)
    return jax.shard_map(step, mesh=mesh, in_specs=in_specs, out_specs=out_specs, check_vma=False)
```
